512 devices in a mesh: pix: 32 (over x, y), tm: 16 (over z, core).
Axes of the slice: x: 4, y: 8, z: 8, core: 2. Of those that a mesh axis runs over, the one named last changes fastest.
Arguments:
- movie_frames: bfloat16 [128, 1024, 4096], P('tm', 'pix'), may hold values from -48 to 48
- depth_index: int32 [1024], P('pix'), may hold values from 0 to 5
- depth_width: float32 [6], replicated, may hold values from 0.7 to 3
- temporal_test_matrix: float32 [128, 96], replicated, may hold values from -4 to 4
- merge_probe: float32 [192, 96], replicated, may hold values from -4 to 4
Outputs:
- temporal_rows: float32 [96, 128], P(None, 'tm')
- loadings: bfloat16 [96, 1024, 4096], P(None, 'pix', 'tm')
The draws below stay inside these ranges and needn't reach their ends.
All inputs are finite; a program needn't handle non-finite values.
Results may differ from the reference program's by a relative error of at most 0.0062.
Values may be sent and summed in bfloat16 or wider, within the bound.
No kernel may reach another device: no remote copies, remote signals or barrier semaphores. Data moves between devices by JAX's collectives and lax.ppermute only.
A program may use at most 64 MiB of HBM per device.

```python
import math
import jax
import jax.numpy as jnp
from jax import lax

ROWS_DEV = 32
COLS = 4096
FRAMES = 128
RANK = 96
HW = 4
NDEPTH = 6
ROWS = 1024
N_PIX = 32


def draw_movie_frames(key, part):
    key_base, key_frame, key_col, key_row = jax.random.split(key, 4)
    tile_count = ROWS // ROWS_DEV
    frame_scale = jnp.exp(jax.random.uniform(key_frame, (FRAMES, tile_count, 1, 1), jnp.float32, 0.0, math.log(3.0)))
    frame_scale = jnp.broadcast_to(frame_scale, (FRAMES, tile_count, ROWS_DEV, 1)).reshape(FRAMES, ROWS, 1)
    col_scale = jnp.exp(jax.random.uniform(key_col, (1, 1, COLS), jnp.float32, 0.0, math.log(2.0)))
    row_scale = jnp.exp(jax.random.uniform(key_row, (1, ROWS, 1), jnp.float32, 0.0, math.log(2.0)))
    base_values = jax.random.truncated_normal(key_base, -4.0, 4.0, (FRAMES, ROWS, COLS), jnp.float32)
    return (base_values * frame_scale * col_scale * row_scale).astype(jnp.bfloat16)


def touch_ends(values, key, least, top_value):
    index_at = [jax.random.randint(jax.random.fold_in(key, axis), (), 0, length) for axis, length in enumerate(values.shape)]
    longest = values.shape.index(max(values.shape))
    neighbour = index_at[:longest] + [(index_at[longest] + 1) % values.shape[longest]] + index_at[longest + 1:]
    return values.at[tuple(index_at)].set(least).at[tuple(neighbour)].set(top_value)


def normal_values(rng, dims, scale, bound, kind=jnp.bfloat16):
    drawn = jax.random.normal(rng, dims, jnp.float32) * scale
    return jnp.minimum(jnp.maximum(drawn, -bound), bound).astype(kind)


def setup_inputs(seed: int = 0) -> dict:
    splits = jax.random.split(jax.random.key(seed), 6)
    return {
        "movie_frames": draw_movie_frames(jax.random.fold_in(splits[5], 71), 0),
        "depth_index": touch_ends(jax.random.randint(splits[1], (ROWS,), 0, NDEPTH), jax.random.fold_in(splits[1], 1), 0, NDEPTH - 1).astype(jnp.int32),
        "depth_width": jnp.clip(jnp.exp(jax.random.uniform(splits[2], (NDEPTH,), jnp.float32, math.log(0.7), math.log(3.0))), 0.7, 3.0),
        "temporal_test_matrix": normal_values(splits[3], (FRAMES, RANK), 1.0, 4.0, jnp.float32),
        "merge_probe": normal_values(splits[4], (2 * RANK, RANK), 1.0, 4.0, jnp.float32),
    }


greatest_rank = lax.Precision.HIGHEST
reduction_multiplier = math.sqrt(0.5)
growth_multiplier = math.sqrt(2.0)

def taps_table(depth_width):
    offsets = jnp.arange(-HW, HW + 1).astype(jnp.float32)
    kernel_raw = jnp.exp(-offsets[None, :] ** 2 / (2.0 * depth_width[:, None] ** 2))
    return kernel_raw / lax.optimization_barrier(jnp.sum(kernel_raw, axis=1, keepdims=True))

def row_weights(row_depth, depth_width):
    classes = jnp.arange(NDEPTH).astype(jnp.int32)
    onehot = (row_depth[:, None] == classes[None, :]).astype(jnp.float32)
    return jnp.dot(onehot, taps_table(depth_width), precision=greatest_rank)

def smooth_rows(padded, weights):
    row_count = weights.shape[0]
    summed = jnp.zeros((padded.shape[0], row_count, padded.shape[2]), jnp.float32)
    for offset in range(2 * HW + 1):
        summed = summed + weights[:, offset][None, :, None] * padded[:, offset:offset + row_count, :].astype(jnp.float32)
    return summed.astype(jnp.bfloat16)

def orthonormal(sketch):
    factor = jnp.linalg.cholesky(jnp.dot(sketch.T, sketch, precision=greatest_rank))
    return lax.linalg.triangular_solve(factor, sketch, left_side=False, lower=True, transpose_a=True)

def tile_basis(scatter_matrix, temporal_test_matrix):
    basis_cols = orthonormal(jnp.dot(scatter_matrix, temporal_test_matrix, precision=greatest_rank))
    projected = jnp.dot(basis_cols.T, scatter_matrix, precision=greatest_rank)
    inner_gram = jnp.dot(projected, basis_cols, precision=greatest_rank)
    factor = jnp.linalg.cholesky(inner_gram)
    coefficient = lax.linalg.triangular_solve(factor, basis_cols, left_side=False, lower=True, transpose_a=True)
    return (factor, projected, coefficient)

def merge_pair(first_rows, second_rows, merge_probe):
    stacked = jnp.concatenate([first_rows, second_rows], axis=0)
    stacked_gram = jnp.dot(stacked, stacked.T, precision=greatest_rank)
    rotation = orthonormal(jnp.dot(stacked_gram, merge_probe, precision=greatest_rank))
    merged = jnp.dot(rotation.T, stacked, precision=greatest_rank) * reduction_multiplier
    return (merged, rotation)

def merge_tree(tile_rows, merge_probe):
    tile_total, rank_count, frame_count = tile_rows.shape
    route_list = jnp.broadcast_to(jnp.eye(rank_count, dtype=jnp.float32), (tile_total, rank_count, rank_count))
    tile_ids = jnp.arange(tile_total).astype(jnp.int32)
    current = tile_rows
    for merge_level in range(tile_total.bit_length() - 1):
        group_count = current.shape[0] // 2
        paired = current.reshape(group_count, 2, rank_count, frame_count)
        merged, rotation = jax.vmap(merge_pair, in_axes=(0, 0, None))(paired[:, 0], paired[:, 1], merge_probe)
        blocks = rotation.reshape(group_count, 2, rank_count, rank_count) * growth_multiplier
        node_ids = tile_ids >> merge_level
        selected_columns = blocks[node_ids >> 1, node_ids & 1]
        route_list = jnp.einsum('ope,oeg->opg', route_list, selected_columns, precision=greatest_rank)
        current = merged
    return (current[0], route_list)

def reference(movie_frames, depth_index, depth_width, temporal_test_matrix, merge_probe):
    padded_movie = jnp.pad(movie_frames, ((0, 0), (HW, HW), (0, 0)))

    def tile_smooth(tile_index):
        start = (tile_index * ROWS_DEV).astype(jnp.int32)
        block_rows = lax.dynamic_slice_in_dim(padded_movie, start, ROWS_DEV + 2 * HW, 1)
        row_depth = lax.dynamic_slice_in_dim(depth_index, start, ROWS_DEV, 0)
        smoothed = smooth_rows(block_rows, row_weights(row_depth, depth_width))
        return smoothed.reshape(FRAMES, ROWS_DEV * COLS)

    def tile_front(tile_index):
        flattened = tile_smooth(tile_index)
        partial_cov = lax.dot_general(flattened.astype(jnp.float32), flattened.astype(jnp.float32), (((1,), (1,)), ((), ())), preferred_element_type=jnp.float32)
        scatter_matrix = partial_cov / (ROWS_DEV * COLS)
        factor, projected, coefficient = tile_basis(scatter_matrix, temporal_test_matrix)
        own_rows = lax.linalg.triangular_solve(factor, projected, left_side=True, lower=True)
        return (own_rows, coefficient)
    tile_numbers = jnp.arange(N_PIX).astype(jnp.int32)
    tile_rows, coefficients = lax.map(tile_front, tile_numbers)
    root_rows, route_list = merge_tree(tile_rows, merge_probe)

    def tile_back(inputs):
        tile_index, coefficient, path_product = inputs
        flattened = tile_smooth(tile_index)
        weights_table = jnp.dot(coefficient, path_product, precision=greatest_rank).astype(jnp.bfloat16)
        loading_flat = lax.dot_general(weights_table.astype(jnp.float32), flattened.astype(jnp.float32), (((0,), (0,)), ((), ())), preferred_element_type=jnp.float32)
        return loading_flat.astype(jnp.bfloat16).reshape(RANK, ROWS_DEV, COLS)
    tile_loadings = lax.map(tile_back, (tile_numbers, coefficients, route_list))
    loadings = jnp.transpose(tile_loadings, (1, 0, 2, 3)).reshape(RANK, ROWS, COLS)
    return (root_rows, loadings)
```

```python
import math

import jax
import jax.numpy as jnp
from jax import lax
from jax.experimental import pallas as pl
from jax.experimental.pallas import tpu as pltpu
from jax.sharding import PartitionSpec as P

ROWS_DEV = 32
COLS = 4096
FRAMES = 128
RANK = 96
HW = 4
NDEPTH = 6
BLOCK = 8

highest = lax.Precision.HIGHEST
reduction_multiplier = math.sqrt(0.5)
growth_multiplier = math.sqrt(2.0)
vmem = pl.BlockSpec(memory_space=pltpu.VMEM)
smem = pl.BlockSpec(memory_space=pltpu.SMEM)


def taps_table(depth_width):
    offsets = jnp.arange(-HW, HW + 1).astype(jnp.float32)
    kernel_raw = jnp.exp(-offsets[None, :] ** 2 / (2.0 * depth_width[:, None] ** 2))
    return kernel_raw / jnp.sum(kernel_raw, axis=1, keepdims=True)


def row_weights(row_depth, depth_width):
    classes = jnp.arange(NDEPTH)
    onehot = (row_depth[:, None] == classes[None, :]).astype(jnp.float32)
    return jnp.dot(onehot, taps_table(depth_width), precision=highest)


def split_bf16(value):
    high = lax.reduce_precision(value, exponent_bits=8, mantissa_bits=7)
    return high.astype(jnp.bfloat16), (value - high).astype(jnp.bfloat16)


def smoothing_matrices(weights, frames):
    rows = ROWS_DEV * frames
    spread = jnp.repeat(weights, frames, axis=0)
    out_row = (jnp.arange(rows) // frames)[:, None]
    out_frame = (jnp.arange(rows) % frames)[:, None]
    halo = jnp.arange(2 * frames * HW)
    frame_in = jnp.concatenate([jnp.arange(rows) // ROWS_DEV, halo // HW % frames])[None, :]
    row_in = jnp.concatenate(
        [jnp.arange(rows) % ROWS_DEV + HW, halo % HW + jnp.where(halo < frames * HW, 0, HW + ROWS_DEV)]
    )[None, :]
    tap = jnp.where(frame_in == out_frame, row_in - out_row, -1)
    matrix = jnp.zeros(tap.shape, jnp.float32)
    for offset in range(2 * HW + 1):
        matrix = matrix + jnp.where(tap == offset, spread[:, offset : offset + 1], 0.0)
    return split_bf16(matrix)


def dot_bf16(left, right):
    return lax.dot_general(left, right, (((1,), (0,)), ((), ())), preferred_element_type=jnp.float32)


def smooth_kernel(movie_ref, low_ref, high_ref, coarse_ref, fine_ref, out_ref):
    frames, rows, cols = movie_ref.shape
    movie = movie_ref[...].reshape(frames * rows, cols)
    halo = jnp.concatenate([low_ref[...], high_ref[...]], axis=0)
    data = jnp.concatenate([movie, halo], axis=0)
    out_ref[0] = (dot_bf16(coarse_ref[...], data) + dot_bf16(fine_ref[...], data)).astype(jnp.bfloat16)


def smooth_tile(movie, low, high, coarse, fine, parts):
    frames = movie.shape[0]
    width = COLS // parts
    rows = frames * ROWS_DEV
    halo = pl.BlockSpec((frames * HW, width), lambda i: (0, i))
    matrix = pl.BlockSpec(coarse.shape, lambda i: (0, 0))
    return pl.pallas_call(
        smooth_kernel,
        grid=(parts,),
        in_specs=[pl.BlockSpec((frames, ROWS_DEV, width), lambda i: (0, 0, i)), halo, halo, matrix, matrix],
        out_specs=pl.BlockSpec((1, rows, width), lambda i: (i, 0, 0)),
        out_shape=jax.ShapeDtypeStruct((parts, rows, width), jnp.bfloat16),
        name="smooth",
    )(movie, low, high, coarse, fine)


def spread_selector(parity, frames):
    row = lax.broadcasted_iota(jnp.int32, (2 * FRAMES, FRAMES), 0)
    col = lax.broadcasted_iota(jnp.int32, (2 * FRAMES, FRAMES), 1)
    wanted = col // frames * (2 * frames) + parity * frames + col % frames
    return row == wanted


def covariance_kernel(data_ref, out_ref, total_ref):
    step = pl.program_id(0)
    parts, pair, width = data_ref.shape
    frames = pair // 2

    @pl.when(step == 0)
    def _():
        total_ref[...] = jnp.zeros_like(total_ref)

    data = data_ref[...].reshape(parts * pair, width)
    total_ref[...] += lax.dot_general(data, data, (((1,), (1,)), ((), ())), preferred_element_type=jnp.float32)

    @pl.when(step == pl.num_programs(0) - 1)
    def _():
        total = total_ref[...].reshape(parts, 2, frames, parts * pair)
        result = None
        for parity in range(2):
            rows = total[:, parity].reshape(parts * frames, parts * pair)
            selector = jnp.where(spread_selector(parity, frames), 1.0, 0.0)
            term = jnp.dot(rows, selector, precision=highest, preferred_element_type=jnp.float32)
            result = term if result is None else result + term
        out_ref[...] = result


def covariance_part(columns):
    parts, rows, width = columns.shape
    pair = 2 * rows // ROWS_DEV
    return pl.pallas_call(
        covariance_kernel,
        grid=(rows // pair,),
        in_specs=[pl.BlockSpec((parts, pair, width), lambda i: (0, i, 0))],
        out_specs=pl.BlockSpec((FRAMES, FRAMES), lambda i: (0, 0)),
        out_shape=jax.ShapeDtypeStruct((FRAMES, FRAMES), jnp.float32),
        scratch_shapes=[pltpu.VMEM((2 * FRAMES, 2 * FRAMES), jnp.float32)],
        name="covariance",
    )(columns)


def loading_kernel(weights_ref, data_ref, out_ref, matrix_ref):
    parts, pair, width = data_ref.shape
    frames = pair // 2

    @pl.when(pl.program_id(0) == 0)
    def _():
        weights = weights_ref[...].astype(jnp.bfloat16)
        for parity in range(2):
            selector = jnp.where(spread_selector(parity, frames), 1.0, 0.0).astype(jnp.bfloat16)
            spread = lax.dot_general(
                weights, selector, (((1,), (1,)), ((), ())), preferred_element_type=jnp.float32
            )
            matrix_ref[parity * RANK : (parity + 1) * RANK, :] = spread.astype(jnp.bfloat16)

    data = data_ref[...].reshape(parts * pair, width)
    result = dot_bf16(matrix_ref[...], data).astype(jnp.bfloat16)
    out_ref[0] = result[:RANK]
    out_ref[1] = result[RANK:]


def loading_rows(weights, columns):
    parts, rows, width = columns.shape
    pair = 2 * rows // ROWS_DEV
    return pl.pallas_call(
        loading_kernel,
        grid=(rows // pair,),
        in_specs=[
            pl.BlockSpec((RANK, FRAMES), lambda i: (0, 0)),
            pl.BlockSpec((parts, pair, width), lambda i: (0, i, 0)),
        ],
        out_specs=pl.BlockSpec((2, RANK, width), lambda i: (i, 0, 0)),
        out_shape=jax.ShapeDtypeStruct((ROWS_DEV, RANK, width), jnp.bfloat16),
        scratch_shapes=[pltpu.VMEM((2 * RANK, 2 * FRAMES), jnp.bfloat16)],
        name="loadings",
    )(weights, columns)


def transposed_dot(left, right):
    return lax.dot_general(
        left, right, (((0,), (0,)), ((), ())), precision=highest, preferred_element_type=jnp.float32
    )


def plain_dot(left, right):
    return jnp.dot(left, right, precision=highest, preferred_element_type=jnp.float32)


def solve_with_factor(system):
    size = system.shape[0]
    width = system.shape[1]
    lanes = 128
    sub = lax.broadcasted_iota(jnp.int32, (BLOCK, 1), 0)
    current = system
    done = []
    for start in range(0, size, BLOCK):
        panel = current[:BLOCK]
        a = {}
        for i in range(BLOCK):
            for j in range(i + 1):
                a[i, j] = jnp.broadcast_to(panel[j : j + 1, start + i : start + i + 1], (BLOCK, lanes))
        factor = {}
        inverse_diag = []
        for j in range(BLOCK):
            root = lax.rsqrt(a[j, j])
            inverse_diag.append(root)
            for i in range(j + 1, BLOCK):
                factor[i, j] = a[i, j] * root
            for i in range(j + 1, BLOCK):
                for k in range(j + 1, i + 1):
                    a[i, k] = a[i, k] - factor[i, j] * factor[k, j]
        inverse = {}
        for j in range(BLOCK):
            inverse[j, j] = inverse_diag[j]
            for i in range(j + 1, BLOCK):
                total = factor[i, j] * inverse[j, j]
                for k in range(j + 1, i):
                    total = total + factor[i, k] * inverse[k, j]
                inverse[i, j] = -total * inverse_diag[i]
        solved = None
        for j in range(BLOCK):
            column = jnp.where(sub == j, inverse[j, j], 0.0)
            for i in range(j + 1, BLOCK):
                column = jnp.where(sub == i, inverse[i, j], column)
            term = jnp.concatenate([column] * (width // lanes), axis=1) * jnp.broadcast_to(
                panel[j : j + 1], (BLOCK, width)
            )
            solved = term if solved is None else solved + term
        done.append(solved[:, lanes:])
        if start + BLOCK < size:
            update = transposed_dot(solved[:, :lanes], solved)
            current = current[BLOCK:] - update[start + BLOCK : size]
    return jnp.concatenate(done, axis=0)


def basis_kernel(covariance_ref, test_ref, rows_ref, weights_ref):
    covariance = covariance_ref[...] * (1.0 / (ROWS_DEV * COLS))
    sketch = plain_dot(covariance, test_ref[...])
    image = plain_dot(covariance, sketch)
    row = lax.broadcasted_iota(jnp.int32, (FRAMES, FRAMES), 0)
    col = lax.broadcasted_iota(jnp.int32, (FRAMES, FRAMES), 1)
    identity = jnp.where(row == col, 1.0, 0.0)
    system = transposed_dot(sketch, jnp.concatenate([image, covariance, identity], axis=1))
    solved = solve_with_factor(system[:RANK])
    rows_ref[...] = solved[:, :FRAMES]
    weights_ref[...] = solved[:, FRAMES:]


def tile_basis(covariance, test_matrix):
    shape = jax.ShapeDtypeStruct((RANK, FRAMES), jnp.float32)
    return pl.pallas_call(
        basis_kernel,
        in_specs=[vmem, vmem],
        out_specs=[vmem, vmem],
        out_shape=[shape, shape],
        name="basis",
    )(covariance, test_matrix)


def merge_kernel(first_ref, own_ref, partner_ref, weights_ref, probe_ref, rows_ref, new_weights_ref):
    is_first = first_ref[0] == 1
    own = own_ref[...]
    partner = partner_ref[...]
    weights = weights_ref[...]
    stacked = jnp.concatenate([jnp.where(is_first, own, partner), jnp.where(is_first, partner, own)], axis=0)
    placed = jnp.concatenate([jnp.where(is_first, weights, 0.0), jnp.where(is_first, 0.0, weights)], axis=0)
    sketch = plain_dot(stacked, transposed_dot(stacked, probe_ref[...]))
    system = transposed_dot(sketch, jnp.concatenate([sketch, stacked, placed], axis=1))
    solved = solve_with_factor(system[:RANK])
    rows_ref[...] = solved[:, :FRAMES] * reduction_multiplier
    new_weights_ref[...] = solved[:, FRAMES:] * growth_multiplier


def merge(is_first, own, partner, weights, probe):
    shape = jax.ShapeDtypeStruct((RANK, FRAMES), jnp.float32)
    return pl.pallas_call(
        merge_kernel,
        in_specs=[smem, vmem, vmem, vmem, vmem],
        out_specs=[vmem, vmem],
        out_shape=[shape, shape],
        name="merge",
    )(is_first, own, partner, weights, probe)


def sum_over_tm(partial):
    parts = lax.axis_size("tm")
    height = partial.shape[0] // parts
    pieces = lax.all_to_all(partial.reshape(parts, height, -1), "tm", 0, 0, tiled=True)
    own = jnp.sum(pieces, axis=0, keepdims=True)
    whole = lax.all_to_all(jnp.broadcast_to(own, pieces.shape), "tm", 0, 0, tiled=True)
    return whole.reshape(partial.shape)


def body(movie_frames, depth_index, depth_width, temporal_test_matrix, merge_probe):
    frames = movie_frames.shape[0]
    parts = lax.axis_size("tm")
    count = lax.axis_size("pix")
    forward = [(i, i + 1) for i in range(count - 1)]
    backward = [(target, source) for source, target in forward]
    low = lax.ppermute(movie_frames[:, ROWS_DEV - HW :].reshape(frames * HW, COLS), "pix", forward)
    high = lax.ppermute(movie_frames[:, :HW].reshape(frames * HW, COLS), "pix", backward)
    coarse, fine = smoothing_matrices(row_weights(depth_index, depth_width), frames)
    smoothed = smooth_tile(movie_frames, low, high, coarse, fine, parts)
    columns = lax.all_to_all(smoothed, "tm", 0, 0, tiled=True)
    covariance = sum_over_tm(covariance_part(columns))
    spare = FRAMES - RANK
    test_matrix = jnp.pad(temporal_test_matrix, ((0, 0), (0, spare)))
    probe = jnp.pad(merge_probe, ((0, 0), (0, spare)))
    own_rows, weights = tile_basis(covariance, test_matrix)
    position = lax.axis_index("pix")
    for level in range(count.bit_length() - 1):
        pairs = [(source, source ^ (1 << level)) for source in range(count)]
        partner = lax.ppermute(own_rows, "pix", pairs)
        is_first = (1 - (position >> level & 1)).astype(jnp.int32).reshape(1)
        own_rows, weights = merge(is_first, own_rows, partner, weights, probe)
    loadings = jnp.transpose(loading_rows(weights, columns), (1, 0, 2))
    own_times = lax.dynamic_slice_in_dim(own_rows, lax.axis_index("tm") * frames, frames, 1)
    return (own_times, loadings)


def solution(mesh):
    in_specs = (P("tm", "pix", None), P("pix"), P(), P(), P())
    out_specs = (P(None, "tm"), P(None, "pix", "tm"))
    return jax.shard_map(body, mesh=mesh, in_specs=in_specs, out_specs=out_specs, check_vma=False)
```

```python
import math

import jax
import jax.numpy as jnp
from jax import lax
from jax.experimental import pallas as pl
from jax.experimental.pallas import tpu as pltpu
from jax.sharding import PartitionSpec as P

ROWS_DEV = 32
COLS = 4096
FRAMES = 128
RANK = 96
HW = 4
NDEPTH = 6
BLOCK = 8
SMOOTH_GROUP = 4
PAIR_GROUP = 4
LOADING_ROWS = 8

highest = lax.Precision.HIGHEST
reduction_multiplier = math.sqrt(0.5)
growth_multiplier = math.sqrt(2.0)
vmem = pl.BlockSpec(memory_space=pltpu.VMEM)
smem = pl.BlockSpec(memory_space=pltpu.SMEM)


def near(*values):
    return [pltpu.with_memory_space_constraint(value, pltpu.VMEM) for value in values]


def taps_table(depth_width):
    offsets = jnp.arange(-HW, HW + 1).astype(jnp.float32)
    kernel_raw = jnp.exp(-offsets[None, :] ** 2 / (2.0 * depth_width[:, None] ** 2))
    return kernel_raw / jnp.sum(kernel_raw, axis=1, keepdims=True)


def row_weights(row_depth, depth_width):
    classes = jnp.arange(NDEPTH)
    onehot = (row_depth[:, None] == classes[None, :]).astype(jnp.float32)
    return jnp.dot(onehot, taps_table(depth_width), precision=highest)


def split_bf16(value):
    high = lax.reduce_precision(value, exponent_bits=8, mantissa_bits=7)
    return high.astype(jnp.bfloat16), (value - high).astype(jnp.bfloat16)


def smoothing_matrices(weights, frames):
    rows = ROWS_DEV * frames
    spread = jnp.repeat(weights, frames, axis=0)
    out_row = (jnp.arange(rows) // frames)[:, None]
    out_frame = (jnp.arange(rows) % frames)[:, None]
    halo = jnp.arange(2 * frames * HW)
    frame_in = jnp.concatenate([jnp.arange(rows) // ROWS_DEV, halo // HW % frames])[None, :]
    row_in = jnp.concatenate(
        [jnp.arange(rows) % ROWS_DEV + HW, halo % HW + jnp.where(halo < frames * HW, 0, HW + ROWS_DEV)]
    )[None, :]
    tap = jnp.where(frame_in == out_frame, row_in - out_row, -1)
    matrix = jnp.zeros(tap.shape, jnp.float32)
    for offset in range(2 * HW + 1):
        matrix = matrix + jnp.where(tap == offset, spread[:, offset : offset + 1], 0.0)
    high, low = split_bf16(matrix)
    return jnp.concatenate([high, low], axis=0)


def dot_bf16(left, right):
    return lax.dot_general(left, right, (((1,), (0,)), ((), ())), preferred_element_type=jnp.float32)


def smooth_kernel(movie_ref, low_ref, high_ref, matrix_ref, out_ref):
    frames, rows, cols = movie_ref.shape
    count, out_rows, width = out_ref.shape
    start = pl.program_id(0) * cols
    matrix = matrix_ref[...]
    for part in range(count):
        movie = movie_ref[:, :, part * width : (part + 1) * width].reshape(frames * rows, width)
        lanes = pl.ds(pl.multiple_of(start + part * width, width), width)
        data = jnp.concatenate([movie, low_ref[:, lanes], high_ref[:, lanes]], axis=0)
        both = dot_bf16(matrix, data)
        out_ref[part] = (both[:out_rows] + both[out_rows:]).astype(jnp.bfloat16)


def smooth_tile(movie, low, high, matrix, parts):
    frames = movie.shape[0]
    width = COLS // parts
    rows = frames * ROWS_DEV
    group = SMOOTH_GROUP
    return pl.pallas_call(
        smooth_kernel,
        grid=(parts // group,),
        in_specs=[
            pl.BlockSpec((frames, ROWS_DEV, group * width), lambda i: (0, 0, i)),
            vmem,
            vmem,
            vmem,
        ],
        out_specs=pl.BlockSpec((group, rows, width), lambda i: (i, 0, 0)),
        out_shape=jax.ShapeDtypeStruct((parts, rows, width), jnp.bfloat16),
        name="smooth",
    )(movie, *near(low, high, matrix))


def spread_selector(parity, frames):
    row = lax.broadcasted_iota(jnp.int32, (2 * FRAMES, FRAMES), 0)
    col = lax.broadcasted_iota(jnp.int32, (2 * FRAMES, FRAMES), 1)
    wanted = col // frames * (2 * frames) + parity * frames + col % frames
    return row == wanted


def covariance_kernel(data_ref, out_ref, total_ref):
    step = pl.program_id(0)
    parts, rows, width = data_ref.shape
    pair = rows // PAIR_GROUP
    frames = pair // 2

    @pl.when(step == 0)
    def _():
        total_ref[...] = jnp.zeros_like(total_ref)

    pieces = [
        data_ref[:, i * pair : (i + 1) * pair, :].reshape(parts * pair, width) for i in range(PAIR_GROUP)
    ]
    data = jnp.concatenate(pieces, axis=1)
    total_ref[...] += lax.dot_general(data, data, (((1,), (1,)), ((), ())), preferred_element_type=jnp.float32)

    @pl.when(step == pl.num_programs(0) - 1)
    def _():
        total = total_ref[...].reshape(parts, 2, frames, parts * pair)
        result = None
        for parity in range(2):
            rows = total[:, parity].reshape(parts * frames, parts * pair)
            selector = jnp.where(spread_selector(parity, frames), 1.0, 0.0)
            term = jnp.dot(rows, selector, precision=highest, preferred_element_type=jnp.float32)
            result = term if result is None else result + term
        out_ref[...] = result


def covariance_part(columns):
    parts, rows, width = columns.shape
    block = PAIR_GROUP * 2 * rows // ROWS_DEV
    return pl.pallas_call(
        covariance_kernel,
        grid=(rows // block,),
        in_specs=[pl.BlockSpec((parts, block, width), lambda i: (0, i, 0))],
        out_specs=pl.BlockSpec((FRAMES, FRAMES), lambda i: (0, 0)),
        out_shape=pltpu.VMEM((FRAMES, FRAMES), jnp.float32),
        scratch_shapes=[pltpu.VMEM((2 * FRAMES, 2 * FRAMES), jnp.float32)],
        name="covariance",
    )(columns)


def loading_kernel(weights_ref, data_ref, out_ref, matrix_ref, turn_ref):
    rank, height, width = out_ref.shape
    parts, rows, _ = data_ref.shape
    frames = rows // height
    pair = 2 * frames

    @pl.when(pl.program_id(0) == 0)
    def _():
        weights = weights_ref[...].astype(jnp.bfloat16)
        for parity in range(2):
            selector = jnp.where(spread_selector(parity, frames), 1.0, 0.0).astype(jnp.bfloat16)
            spread = lax.dot_general(
                weights, selector, (((1,), (1,)), ((), ())), preferred_element_type=jnp.float32
            )
            matrix_ref[parity * rank : (parity + 1) * rank, :] = spread.astype(jnp.bfloat16)

    matrix = matrix_ref[...]
    for i in range(height // 2):
        data = data_ref[:, i * pair : (i + 1) * pair, :].reshape(parts * pair, width)
        result = dot_bf16(matrix, data)
        for parity in range(2):
            for half in range(width // 128):
                lanes = slice(half * 128, (half + 1) * 128)
                turn_ref[half, pl.ds(2 * i + parity, rank, stride=height), :] = result[
                    parity * rank : (parity + 1) * rank, lanes
                ]
    for half in range(width // 128):
        lanes = slice(half * 128, (half + 1) * 128)
        out_ref[:, :, lanes] = turn_ref[half].reshape(rank, height, 128).astype(jnp.bfloat16)


def loading_rows(weights, columns):
    parts, rows, width = columns.shape
    height = LOADING_ROWS
    return pl.pallas_call(
        loading_kernel,
        grid=(ROWS_DEV // height,),
        in_specs=[vmem, pl.BlockSpec((parts, height * (rows // ROWS_DEV), width), lambda i: (0, i, 0))],
        out_specs=pl.BlockSpec((RANK, height, width), lambda i: (0, i, 0)),
        out_shape=jax.ShapeDtypeStruct((RANK, ROWS_DEV, width), jnp.bfloat16),
        scratch_shapes=[
            pltpu.VMEM((2 * RANK, 2 * FRAMES), jnp.bfloat16),
            pltpu.VMEM((width // 128, RANK * height, 128), jnp.float32),
        ],
        name="loadings",
    )(*near(weights), columns)


def split_in_three(value):
    high = value.astype(jnp.bfloat16).astype(jnp.float32)
    rest = value - high
    middle = rest.astype(jnp.bfloat16).astype(jnp.float32)
    return high, middle, rest - middle


def exact_dot(left, right):
    rows = left.shape[0]
    high, middle, low = [part.astype(jnp.bfloat16) for part in split_in_three(left)]
    right_high, right_middle, right_low = [part.astype(jnp.bfloat16) for part in split_in_three(right)]
    first = dot_bf16(jnp.concatenate([high, middle, low], axis=0), right_high)
    second = dot_bf16(jnp.concatenate([high, middle], axis=0), right_middle)
    third = dot_bf16(high, right_low)
    small = first[2 * rows :] + (second[rows:] + third)
    return first[:rows] + (first[rows : 2 * rows] + second[:rows] + small)


def solve_with_factor(system):
    size, width = system.shape
    lanes = 128
    sub = lax.broadcasted_iota(jnp.int32, (BLOCK, lanes), 0)

    def wide(value):
        return jnp.concatenate([value] * (width // lanes), axis=1)

    def spread_row(value, j):
        return jnp.broadcast_to(value[j : j + 1], value.shape)

    def spread_columns(value, start):
        return [
            jnp.broadcast_to(value[:, start + k : start + k + 1], (BLOCK, lanes)) for k in range(BLOCK)
        ]

    panel = system[:BLOCK]
    rest = system[BLOCK:]
    done = []
    for start in range(0, size, BLOCK):
        after = start + BLOCK
        last = after == size
        columns = spread_columns(panel, start)
        if not last:
            following = rest[:BLOCK]
            next_columns = spread_columns(following, start)
        scale = None
        for j in range(BLOCK):
            root = lax.rsqrt(spread_row(columns[j], j))
            inverse = root * root
            for k in range(j + 1, BLOCK):
                ratio = spread_row(columns[j], k) * inverse
                columns[k] = columns[k] - columns[j] * ratio
                if not last:
                    next_columns[k] = next_columns[k] - next_columns[j] * ratio
            pivot_row = spread_row(panel, j) * wide(inverse)
            if j < BLOCK - 1:
                panel = panel - wide(jnp.where(sub > j, columns[j], 0.0)) * pivot_row
            if not last:
                following = following - wide(next_columns[j]) * pivot_row
            scale = root if scale is None else jnp.where(sub == j, root, scale)
        solved = panel * wide(scale)
        done.append(solved[:, lanes:])
        if last:
            break
        panel = following
        if after + BLOCK < size:
            high, middle, low = split_in_three(solved)
            left = jnp.concatenate([x[:, :lanes] for x in (high, high, middle, high, middle, low)], axis=0)
            left = left.T[after + BLOCK : size].astype(jnp.bfloat16)
            right = jnp.concatenate([high, middle, high, low, middle, high], axis=0).astype(jnp.bfloat16)
            rest = rest[BLOCK:] - dot_bf16(left, right)
    return jnp.concatenate(done, axis=0)


def basis_kernel(covariance_ref, test_ref, rows_ref, weights_ref):
    covariance = covariance_ref[...] * (1.0 / (ROWS_DEV * COLS))
    sketch = exact_dot(covariance, test_ref[...])
    image = exact_dot(covariance, sketch)
    turned = sketch.T[:RANK]
    system = exact_dot(turned, jnp.concatenate([image, covariance], axis=1))
    solved = solve_with_factor(jnp.concatenate([system, turned], axis=1))
    rows_ref[...] = solved[:, :FRAMES]
    weights_ref[...] = solved[:, FRAMES:]


def tile_basis(covariance, test_matrix):
    shape = pltpu.VMEM((RANK, FRAMES), jnp.float32)
    return pl.pallas_call(
        basis_kernel,
        in_specs=[vmem, vmem],
        out_specs=[vmem, vmem],
        out_shape=[shape, shape],
        name="basis",
    )(*near(covariance, test_matrix))


def merge_kernel(first_ref, own_ref, partner_ref, weights_ref, probe_ref, rows_ref, new_weights_ref):
    is_first = first_ref[0] == 1
    own = own_ref[...]
    partner = partner_ref[...]
    weights = weights_ref[...]
    stacked = jnp.concatenate([jnp.where(is_first, own, partner), jnp.where(is_first, partner, own)], axis=0)
    placed = jnp.concatenate([jnp.where(is_first, weights, 0.0), jnp.where(is_first, 0.0, weights)], axis=0)
    sketch = exact_dot(stacked, exact_dot(stacked.T, probe_ref[...]))
    system = exact_dot(sketch.T[:RANK], jnp.concatenate([sketch, stacked, placed], axis=1))
    solved = solve_with_factor(system)
    rows_ref[...] = solved[:, :FRAMES] * reduction_multiplier
    new_weights_ref[...] = solved[:, FRAMES:] * growth_multiplier


def merge(is_first, own, partner, weights, probe):
    shape = pltpu.VMEM((RANK, FRAMES), jnp.float32)
    return pl.pallas_call(
        merge_kernel,
        in_specs=[smem, vmem, vmem, vmem, vmem],
        out_specs=[vmem, vmem],
        out_shape=[shape, shape],
        name="merge",
    )(is_first, *near(own, partner, weights, probe))


def sum_over_tm(partial):
    parts = lax.axis_size("tm")
    height = partial.shape[0] // parts
    pieces = lax.all_to_all(partial.reshape(parts, height, -1), "tm", 0, 0, tiled=True)
    own = jnp.sum(pieces, axis=0, keepdims=True)
    whole = lax.all_to_all(jnp.broadcast_to(own, pieces.shape), "tm", 0, 0, tiled=True)
    return whole.reshape(partial.shape)


def body(movie_frames, depth_index, depth_width, temporal_test_matrix, merge_probe):
    frames = movie_frames.shape[0]
    parts = lax.axis_size("tm")
    count = lax.axis_size("pix")
    forward = [(i, i + 1) for i in range(count - 1)]
    backward = [(target, source) for source, target in forward]
    low = lax.ppermute(movie_frames[:, ROWS_DEV - HW :].reshape(frames * HW, COLS), "pix", forward)
    high = lax.ppermute(movie_frames[:, :HW].reshape(frames * HW, COLS), "pix", backward)
    matrix = smoothing_matrices(row_weights(depth_index, depth_width), frames)
    smoothed = smooth_tile(movie_frames, low, high, matrix, parts)
    columns = lax.all_to_all(smoothed, "tm", 0, 0, tiled=True)
    covariance = sum_over_tm(covariance_part(columns))
    spare = FRAMES - RANK
    test_matrix = jnp.pad(temporal_test_matrix, ((0, 0), (0, spare)))
    probe = jnp.pad(merge_probe, ((0, 0), (0, spare)))
    own_rows, weights = tile_basis(covariance, test_matrix)
    position = lax.axis_index("pix")
    for level in range(count.bit_length() - 1):
        pairs = [(source, source ^ (1 << level)) for source in range(count)]
        partner = lax.ppermute(own_rows, "pix", pairs)
        is_first = (1 - (position >> level & 1)).astype(jnp.int32).reshape(1)
        own_rows, weights = merge(is_first, own_rows, partner, weights, probe)
    loadings = loading_rows(weights, columns)
    own_times = lax.dynamic_slice_in_dim(own_rows, lax.axis_index("tm") * frames, frames, 1)
    return (own_times, loadings)


def solution(mesh):
    in_specs = (P("tm", "pix", None), P("pix"), P(), P(), P())
    out_specs = (P(None, "tm"), P(None, "pix", "tm"))
    return jax.shard_map(body, mesh=mesh, in_specs=in_specs, out_specs=out_specs, check_vma=False)
```

```python
import math

import jax
import jax.numpy as jnp
from jax import lax
from jax.experimental import pallas as pl
from jax.experimental.pallas import tpu as pltpu
from jax.sharding import PartitionSpec as P

ROWS_DEV = 32
COLS = 4096
FRAMES = 128
RANK = 96
HW = 4
NDEPTH = 6
BLOCK = 8
SMOOTH_GROUP = 4
PAIR_GROUP = 4
LOADING_ROWS = 8

highest = lax.Precision.HIGHEST
reduction_multiplier = math.sqrt(0.5)
growth_multiplier = math.sqrt(2.0)
vmem = pl.BlockSpec(memory_space=pltpu.VMEM)
smem = pl.BlockSpec(memory_space=pltpu.SMEM)


def near(*values):
    return [pltpu.with_memory_space_constraint(value, pltpu.VMEM) for value in values]


def taps_table(depth_width):
    offsets = jnp.arange(-HW, HW + 1).astype(jnp.float32)
    kernel_raw = jnp.exp(-offsets[None, :] ** 2 / (2.0 * depth_width[:, None] ** 2))
    return kernel_raw / jnp.sum(kernel_raw, axis=1, keepdims=True)


def row_weights(row_depth, depth_width):
    classes = jnp.arange(NDEPTH)
    onehot = (row_depth[:, None] == classes[None, :]).astype(jnp.float32)
    return jnp.dot(onehot, taps_table(depth_width), precision=highest)


def split_bf16(value):
    high = lax.reduce_precision(value, exponent_bits=8, mantissa_bits=7)
    return high.astype(jnp.bfloat16), (value - high).astype(jnp.bfloat16)


def smoothing_matrices(weights, frames):
    def matrix(spread, out_row, out_frame, in_row, in_frame):
        tap = jnp.where(in_frame[None, :] == out_frame[:, None], in_row[None, :] - out_row[:, None], -1)
        total = jnp.zeros(tap.shape, jnp.float32)
        for offset in range(2 * HW + 1):
            total = total + jnp.where(tap == offset, spread[:, offset : offset + 1], 0.0)
        high, low = split_bf16(total)
        return jnp.concatenate([high, low], axis=0)

    index = jnp.arange(frames * ROWS_DEV)
    own = matrix(
        jnp.repeat(weights, frames, axis=0),
        index // frames,
        index % frames,
        index % ROWS_DEV + HW,
        index // ROWS_DEV,
    )
    index = jnp.arange(frames * HW)
    edge_rows = index // frames
    sides = [
        matrix(
            jnp.repeat(weights[first : first + HW], frames, axis=0),
            edge_rows + first,
            index % frames,
            index % HW + (first + 2 * HW if first else 0),
            index // HW,
        )
        for first in (0, ROWS_DEV - HW)
    ]
    return own, jnp.concatenate(sides, axis=0)


def dot_bf16(left, right):
    return lax.dot_general(left, right, (((1,), (0,)), ((), ())), preferred_element_type=jnp.float32)


def smooth_kernel(movie_ref, low_ref, high_ref, own_ref, edge_ref, out_ref):
    frames, rows, cols = movie_ref.shape
    count, out_rows, width = out_ref.shape
    start = pl.program_id(0) * cols
    own = own_ref[...]
    edge = edge_ref.shape[0] // 4
    low_matrix = edge_ref[: 2 * edge]
    high_matrix = edge_ref[2 * edge :]
    for part in range(count):
        movie = movie_ref[:, :, part * width : (part + 1) * width].reshape(frames * rows, width)
        lanes = pl.ds(pl.multiple_of(start + part * width, width), width)
        both = dot_bf16(own, movie)
        total = both[:out_rows] + both[out_rows:]
        low = dot_bf16(low_matrix, low_ref[:, lanes])
        high = dot_bf16(high_matrix, high_ref[:, lanes])
        out_ref[part, :edge] = (total[:edge] + (low[:edge] + low[edge:])).astype(jnp.bfloat16)
        out_ref[part, edge : out_rows - edge] = total[edge : out_rows - edge].astype(jnp.bfloat16)
        out_ref[part, out_rows - edge :] = (
            total[out_rows - edge :] + (high[:edge] + high[edge:])
        ).astype(jnp.bfloat16)


def smooth_tile(movie, low, high, matrices, parts):
    frames = movie.shape[0]
    width = COLS // parts
    rows = frames * ROWS_DEV
    group = SMOOTH_GROUP
    return pl.pallas_call(
        smooth_kernel,
        grid=(parts // group,),
        in_specs=[
            pl.BlockSpec((frames, ROWS_DEV, group * width), lambda i: (0, 0, i)),
            vmem,
            vmem,
            vmem,
            vmem,
        ],
        out_specs=pl.BlockSpec((group, rows, width), lambda i: (i, 0, 0)),
        out_shape=jax.ShapeDtypeStruct((parts, rows, width), jnp.bfloat16),
        name="smooth",
    )(movie, *near(low, high, *matrices))


def spread_selector(parity, frames):
    row = lax.broadcasted_iota(jnp.int32, (2 * FRAMES, FRAMES), 0)
    col = lax.broadcasted_iota(jnp.int32, (2 * FRAMES, FRAMES), 1)
    wanted = col // frames * (2 * frames) + parity * frames + col % frames
    return row == wanted


def covariance_kernel(data_ref, out_ref, total_ref):
    step = pl.program_id(0)
    parts, rows, width = data_ref.shape
    pair = rows // PAIR_GROUP
    frames = pair // 2

    @pl.when(step == 0)
    def _():
        total_ref[...] = jnp.zeros_like(total_ref)

    pieces = [
        data_ref[:, i * pair : (i + 1) * pair, :].reshape(parts * pair, width) for i in range(PAIR_GROUP)
    ]
    data = jnp.concatenate(pieces, axis=1)
    total_ref[...] += lax.dot_general(data, data, (((1,), (1,)), ((), ())), preferred_element_type=jnp.float32)

    @pl.when(step == pl.num_programs(0) - 1)
    def _():
        total = total_ref[...].reshape(parts, 2, frames, parts * pair)
        result = None
        for parity in range(2):
            rows = total[:, parity].reshape(parts * frames, parts * pair)
            selector = jnp.where(spread_selector(parity, frames), 1.0, 0.0)
            term = jnp.dot(rows, selector, precision=highest, preferred_element_type=jnp.float32)
            result = term if result is None else result + term
        out_ref[...] = result


def covariance_part(columns):
    parts, rows, width = columns.shape
    block = PAIR_GROUP * 2 * rows // ROWS_DEV
    return pl.pallas_call(
        covariance_kernel,
        grid=(rows // block,),
        in_specs=[pl.BlockSpec((parts, block, width), lambda i: (0, i, 0))],
        out_specs=pl.BlockSpec((FRAMES, FRAMES), lambda i: (0, 0)),
        out_shape=pltpu.VMEM((FRAMES, FRAMES), jnp.float32),
        scratch_shapes=[pltpu.VMEM((2 * FRAMES, 2 * FRAMES), jnp.float32)],
        name="covariance",
    )(columns)


def loading_kernel(weights_ref, data_ref, out_ref, matrix_ref, turn_ref):
    rank, height, width = out_ref.shape
    parts, rows, _ = data_ref.shape
    frames = rows // height
    pair = 2 * frames

    @pl.when(pl.program_id(0) == 0)
    def _():
        weights = weights_ref[...].astype(jnp.bfloat16)
        for parity in range(2):
            selector = jnp.where(spread_selector(parity, frames), 1.0, 0.0).astype(jnp.bfloat16)
            spread = lax.dot_general(
                weights, selector, (((1,), (1,)), ((), ())), preferred_element_type=jnp.float32
            )
            matrix_ref[parity * rank : (parity + 1) * rank, :] = spread.astype(jnp.bfloat16)

    matrix = matrix_ref[...]
    for i in range(height // 2):
        data = data_ref[:, i * pair : (i + 1) * pair, :].reshape(parts * pair, width)
        result = dot_bf16(matrix, data)
        for parity in range(2):
            for half in range(width // 128):
                lanes = slice(half * 128, (half + 1) * 128)
                turn_ref[half, pl.ds(2 * i + parity, rank, stride=height), :] = result[
                    parity * rank : (parity + 1) * rank, lanes
                ]
    for half in range(width // 128):
        lanes = slice(half * 128, (half + 1) * 128)
        out_ref[:, :, lanes] = turn_ref[half].reshape(rank, height, 128).astype(jnp.bfloat16)


def loading_rows(weights, columns):
    parts, rows, width = columns.shape
    height = LOADING_ROWS
    return pl.pallas_call(
        loading_kernel,
        grid=(ROWS_DEV // height,),
        in_specs=[vmem, pl.BlockSpec((parts, height * (rows // ROWS_DEV), width), lambda i: (0, i, 0))],
        out_specs=pl.BlockSpec((RANK, height, width), lambda i: (0, i, 0)),
        out_shape=jax.ShapeDtypeStruct((RANK, ROWS_DEV, width), jnp.bfloat16),
        scratch_shapes=[
            pltpu.VMEM((2 * RANK, 2 * FRAMES), jnp.bfloat16),
            pltpu.VMEM((width // 128, RANK * height, 128), jnp.float32),
        ],
        name="loadings",
    )(*near(weights), columns)


def split_in_three(value):
    high = value.astype(jnp.bfloat16).astype(jnp.float32)
    rest = value - high
    middle = rest.astype(jnp.bfloat16).astype(jnp.float32)
    return high, middle, rest - middle


def exact_dot(left, right):
    rows = left.shape[0]
    high, middle, low = [part.astype(jnp.bfloat16) for part in split_in_three(left)]
    right_high, right_middle, right_low = [part.astype(jnp.bfloat16) for part in split_in_three(right)]
    first = dot_bf16(jnp.concatenate([high, middle, low], axis=0), right_high)
    second = dot_bf16(jnp.concatenate([high, middle], axis=0), right_middle)
    third = dot_bf16(high, right_low)
    small = first[2 * rows :] + (second[rows:] + third)
    return first[:rows] + (first[rows : 2 * rows] + second[:rows] + small)


def solve_with_factors(systems):
    size, width = systems[0].shape
    lanes = 128
    sub = lax.broadcasted_iota(jnp.int32, (BLOCK, lanes), 0)

    def wide(value):
        return jnp.concatenate([value] * (width // lanes), axis=1)

    def spread_row(value, j):
        return jnp.broadcast_to(value[j : j + 1], value.shape)

    def spread_columns(value, start):
        return [
            jnp.broadcast_to(value[:, start + k : start + k + 1], (BLOCK, lanes)) for k in range(BLOCK)
        ]

    total = range(len(systems))
    panel = [system[:BLOCK] for system in systems]
    rest = [system[BLOCK:] for system in systems]
    done = [[] for _ in total]
    for start in range(0, size, BLOCK):
        after = start + BLOCK
        last = after == size
        columns = [spread_columns(panel[i], start) for i in total]
        if not last:
            following = [rest[i][:BLOCK] for i in total]
            next_columns = [spread_columns(following[i], start) for i in total]
        scale = [None for _ in total]
        for j in range(BLOCK):
            for i in total:
                own = columns[i]
                root = lax.rsqrt(spread_row(own[j], j))
                inverse = root * root
                for k in range(j + 1, BLOCK):
                    ratio = spread_row(own[j], k) * inverse
                    own[k] = own[k] - own[j] * ratio
                    if not last:
                        next_columns[i][k] = next_columns[i][k] - next_columns[i][j] * ratio
                pivot_row = spread_row(panel[i], j) * wide(inverse)
                if j < BLOCK - 1:
                    panel[i] = panel[i] - wide(jnp.where(sub > j, own[j], 0.0)) * pivot_row
                if not last:
                    following[i] = following[i] - wide(next_columns[i][j]) * pivot_row
                scale[i] = root if scale[i] is None else jnp.where(sub == j, root, scale[i])
        for i in total:
            solved = panel[i] * wide(scale[i])
            done[i].append(solved[:, lanes:])
            if last:
                continue
            panel[i] = following[i]
            if after + BLOCK < size:
                high, middle, low = split_in_three(solved)
                left = jnp.concatenate(
                    [part[:, :lanes] for part in (high, high, middle, high, middle, low)], axis=0
                )
                left = left.T[after + BLOCK : size].astype(jnp.bfloat16)
                right = jnp.concatenate([high, middle, high, low, middle, high], axis=0)
                rest[i] = rest[i][BLOCK:] - dot_bf16(left, right.astype(jnp.bfloat16))
    return [jnp.concatenate(rows, axis=0) for rows in done]


def store_rows(rows_ref, rows):
    if len(rows_ref.shape) == 2:
        rows_ref[...] = rows
    else:
        for copy in range(rows_ref.shape[0]):
            rows_ref[copy] = rows


def rows_and_weights(copies):
    shape = (RANK, FRAMES) if copies == 1 else (copies, RANK, FRAMES)
    return dict(
        out_specs=[vmem, vmem],
        out_shape=[pltpu.VMEM(shape, jnp.float32), pltpu.VMEM((RANK, FRAMES), jnp.float32)],
    )


def basis_kernel(covariance_ref, test_ref, rows_ref, weights_ref):
    covariance = covariance_ref[...] * (1.0 / (ROWS_DEV * COLS))
    sketch = exact_dot(covariance, test_ref[...])
    image = exact_dot(covariance, sketch)
    turned = sketch.T[:RANK]
    system = exact_dot(turned, jnp.concatenate([image, covariance], axis=1))
    (solved,) = solve_with_factors([jnp.concatenate([system, turned], axis=1)])
    store_rows(rows_ref, solved[:, :FRAMES])
    weights_ref[...] = solved[:, FRAMES:]


def tile_basis(covariance, test_matrix, copies=1):
    return pl.pallas_call(
        basis_kernel, in_specs=[vmem, vmem], name="basis", **rows_and_weights(copies)
    )(*near(covariance, test_matrix))


def merge_nodes(stacks, placed, probe):
    systems = []
    for stacked, weights in zip(stacks, placed):
        sketch = exact_dot(stacked, exact_dot(stacked.T, probe))
        systems.append(exact_dot(sketch.T[:RANK], jnp.concatenate([sketch, stacked, weights], axis=1)))
    solved = solve_with_factors(systems)
    rows = [result[:, :FRAMES] * reduction_multiplier for result in solved]
    weights = sum([result[:, FRAMES:] for result in solved[1:]], solved[0][:, FRAMES:])
    return rows, weights * growth_multiplier


def place(weights, first, second):
    return jnp.concatenate([jnp.where(first, weights, 0.0), jnp.where(second, weights, 0.0)], axis=0)


def merge_kernel(place_ref, own_ref, partner_ref, weights_ref, probe_ref, rows_ref, new_weights_ref):
    is_first = place_ref[0] == 0
    own = own_ref[...]
    partner = partner_ref[...]
    stacked = jnp.concatenate([jnp.where(is_first, own, partner), jnp.where(is_first, partner, own)], axis=0)
    placed = place(weights_ref[...], is_first, jnp.logical_not(is_first))
    (rows,), weights = merge_nodes([stacked], [placed], probe_ref[...])
    store_rows(rows_ref, rows)
    new_weights_ref[...] = weights


def merge(place_in, own, partner, weights, probe, copies=1):
    return pl.pallas_call(
        merge_kernel, in_specs=[smem, vmem, vmem, vmem, vmem], name="merge", **rows_and_weights(copies)
    )(place_in, *near(own, partner, weights, probe))


def merge_four_kernel(place_ref, rows_in_ref, weights_ref, probe_ref, rows_ref, new_weights_ref):
    spot = place_ref[0]
    probe = probe_ref[...]
    weights = weights_ref[...]
    stacks = [rows_in_ref[2 * m : 2 * m + 2].reshape(2 * RANK, FRAMES) for m in range(2)]
    placed = [place(weights, spot == 2 * m, spot == 2 * m + 1) for m in range(2)]
    rows, weights = merge_nodes(stacks, placed, probe)
    (rows,), weights = merge_nodes([jnp.concatenate(rows, axis=0)], [place(weights, spot < 2, spot >= 2)], probe)
    store_rows(rows_ref, rows)
    new_weights_ref[...] = weights


def merge_four(place_in, gathered, weights, probe, copies=1):
    return pl.pallas_call(
        merge_four_kernel, in_specs=[smem, vmem, vmem, vmem], name="merge_four", **rows_and_weights(copies)
    )(place_in, *near(gathered, weights, probe))


def sum_over_tm(partial):
    parts = lax.axis_size("tm")
    height = partial.shape[0] // parts
    pieces = lax.all_to_all(partial.reshape(parts, height, -1), "tm", 0, 0, tiled=True)
    own = jnp.sum(pieces, axis=0, keepdims=True)
    whole = lax.all_to_all(jnp.broadcast_to(own, pieces.shape), "tm", 0, 0, tiled=True)
    return whole.reshape(partial.shape)


def body(movie_frames, depth_index, depth_width, temporal_test_matrix, merge_probe):
    frames = movie_frames.shape[0]
    parts = lax.axis_size("tm")
    count = lax.axis_size("pix")
    forward = [(i, i + 1) for i in range(count - 1)]
    backward = [(target, source) for source, target in forward]
    low = lax.ppermute(movie_frames[:, ROWS_DEV - HW :].reshape(frames * HW, COLS), "pix", forward)
    high = lax.ppermute(movie_frames[:, :HW].reshape(frames * HW, COLS), "pix", backward)
    matrices = smoothing_matrices(row_weights(depth_index, depth_width), frames)
    smoothed = smooth_tile(movie_frames, low, high, matrices, parts)
    columns = lax.all_to_all(smoothed, "tm", 0, 0, tiled=True)
    covariance = sum_over_tm(covariance_part(columns))
    spare = FRAMES - RANK
    test_matrix = jnp.pad(temporal_test_matrix, ((0, 0), (0, spare)))
    probe = jnp.pad(merge_probe, ((0, 0), (0, spare)))
    position = lax.axis_index("pix").astype(jnp.int32)
    levels = count.bit_length() - 1
    sizes = []
    while sum(sizes) < levels:
        sizes.append(2 if levels - sum(sizes) > 1 and sizes[-1:] != [2] else 1)
    copies = [4 if size == 2 else 1 for size in sizes[1:]] + [1]
    rows, weights = tile_basis(covariance, test_matrix, 4 if sizes[0] == 2 else 1)
    level = 0
    for size, next_copies in zip(sizes, copies):
        spot = (position >> level & (2**size - 1)).reshape(1)
        if size == 2:
            step = 1 << level
            groups = [
                [base + k * step for k in range(4)] for base in range(count) if not base & (3 * step)
            ]
            gathered = lax.all_to_all(rows, "pix", 0, 0, tiled=True, axis_index_groups=groups)
            rows, weights = merge_four(spot, gathered, weights, probe, next_copies)
        else:
            pairs = [(source, source ^ (1 << level)) for source in range(count)]
            partner = lax.ppermute(rows, "pix", pairs)
            rows, weights = merge(spot, rows, partner, weights, probe, next_copies)
        level += size
    loadings = loading_rows(weights, columns)
    own_times = lax.dynamic_slice_in_dim(rows, lax.axis_index("tm") * frames, frames, 1)
    return (own_times, loadings)


def solution(mesh):
    in_specs = (P("tm", "pix", None), P("pix"), P(), P(), P())
    out_specs = (P(None, "tm"), P(None, "pix", "tm"))
    return jax.shard_map(body, mesh=mesh, in_specs=in_specs, out_specs=out_specs, check_vma=False)
```

```python
import math

import jax
import jax.numpy as jnp
from jax import lax
from jax.experimental import pallas as pl
from jax.experimental.pallas import tpu as pltpu
from jax.sharding import PartitionSpec as P

ROWS_DEV = 32
COLS = 4096
FRAMES = 128
RANK = 96
HW = 4
NDEPTH = 6
BLOCK = 8
SMOOTH_GROUP = 4
PAIR_GROUP = 4
LOADING_ROWS = 16

highest = lax.Precision.HIGHEST
reduction_multiplier = math.sqrt(0.5)
growth_multiplier = math.sqrt(2.0)
vmem = pl.BlockSpec(memory_space=pltpu.VMEM)
smem = pl.BlockSpec(memory_space=pltpu.SMEM)


def near(*values):
    return [pltpu.with_memory_space_constraint(value, pltpu.VMEM) for value in values]


def taps_table(depth_width):
    offsets = jnp.arange(-HW, HW + 1).astype(jnp.float32)
    kernel_raw = jnp.exp(-offsets[None, :] ** 2 / (2.0 * depth_width[:, None] ** 2))
    return kernel_raw / jnp.sum(kernel_raw, axis=1, keepdims=True)


def row_weights(row_depth, depth_width):
    classes = jnp.arange(NDEPTH)
    onehot = (row_depth[:, None] == classes[None, :]).astype(jnp.float32)
    return jnp.dot(onehot, taps_table(depth_width), precision=highest)


def split_bf16(value):
    high = lax.reduce_precision(value, exponent_bits=8, mantissa_bits=7)
    return high.astype(jnp.bfloat16), (value - high).astype(jnp.bfloat16)


def smoothing_matrices(weights, frames):
    def matrix(spread, out_row, out_frame, in_row, in_frame):
        tap = jnp.where(in_frame[None, :] == out_frame[:, None], in_row[None, :] - out_row[:, None], -1)
        total = jnp.zeros(tap.shape, jnp.float32)
        for offset in range(2 * HW + 1):
            total = total + jnp.where(tap == offset, spread[:, offset : offset + 1], 0.0)
        high, low = split_bf16(total)
        return jnp.concatenate([high, low], axis=0)

    index = jnp.arange(frames * ROWS_DEV)
    own = matrix(
        jnp.repeat(weights, frames, axis=0),
        index // frames,
        index % frames,
        index % ROWS_DEV + HW,
        index // ROWS_DEV,
    )
    index = jnp.arange(frames * HW)
    edge_rows = index // frames
    sides = [
        matrix(
            jnp.repeat(weights[first : first + HW], frames, axis=0),
            edge_rows + first,
            index % frames,
            index % HW + (first + 2 * HW if first else 0),
            index // HW,
        )
        for first in (0, ROWS_DEV - HW)
    ]
    return own, jnp.concatenate(sides, axis=0)


def dot_bf16(left, right):
    return lax.dot_general(left, right, (((1,), (0,)), ((), ())), preferred_element_type=jnp.float32)


def smooth_kernel(movie_ref, own_ref, out_ref, edges_ref):
    frames, rows, _ = movie_ref.shape
    count, out_rows, width = out_ref.shape
    edge = edges_ref.shape[1] // 2
    start = pl.program_id(0) * count
    own = own_ref[...]
    for part in range(count):
        movie = movie_ref[:, :, part * width : (part + 1) * width].reshape(frames * rows, width)
        both = dot_bf16(own, movie)
        total = both[:out_rows] + both[out_rows:]
        out_ref[part] = total.astype(jnp.bfloat16)
        edges_ref[start + part, :edge] = total[:edge]
        edges_ref[start + part, edge:] = total[out_rows - edge :]


def edge_kernel(_, edges_ref, low_ref, high_ref, matrix_ref, out_ref):
    count, edge, width = out_ref.shape
    side = pl.program_id(0)
    rows = pl.ds(pl.multiple_of(side * edge, edge), edge)
    matrix = matrix_ref[pl.ds(pl.multiple_of(side * 2 * edge, 2 * edge), 2 * edge), :]
    for part in range(count):
        lanes = slice(part * width, (part + 1) * width)
        halo = jnp.where(side == 0, low_ref[:, lanes], high_ref[:, lanes])
        both = dot_bf16(matrix, halo)
        out_ref[part] = (edges_ref[part, rows, :] + (both[:edge] + both[edge:])).astype(jnp.bfloat16)


def smooth_tile(movie, low, high, matrices, parts):
    frames = movie.shape[0]
    width = COLS // parts
    rows = frames * ROWS_DEV
    edge = frames * HW
    group = SMOOTH_GROUP
    own, sides = matrices
    shape = jax.ShapeDtypeStruct((parts, rows, width), jnp.bfloat16)
    smoothed, edges = pl.pallas_call(
        smooth_kernel,
        grid=(parts // group,),
        in_specs=[pl.BlockSpec((frames, ROWS_DEV, group * width), lambda i: (0, 0, i)), vmem],
        out_specs=[pl.BlockSpec((group, rows, width), lambda i: (i, 0, 0)), vmem],
        out_shape=[shape, pltpu.VMEM((parts, 2 * edge, width), jnp.float32)],
        name="smooth",
    )(movie, *near(own))
    return pl.pallas_call(
        edge_kernel,
        grid=(2,),
        in_specs=[pl.BlockSpec(memory_space=pl.ANY), vmem, vmem, vmem, vmem],
        out_specs=pl.BlockSpec((parts, edge, width), lambda i: (0, i * (rows // edge - 1), 0)),
        out_shape=shape,
        input_output_aliases={0: 0},
        name="edges",
    )(smoothed, *near(edges, low, high, sides))


def spread_selector(parity, frames):
    row = lax.broadcasted_iota(jnp.int32, (2 * FRAMES, FRAMES), 0)
    col = lax.broadcasted_iota(jnp.int32, (2 * FRAMES, FRAMES), 1)
    wanted = col // frames * (2 * frames) + parity * frames + col % frames
    return row == wanted


def covariance_kernel(data_ref, out_ref, total_ref):
    step = pl.program_id(0)
    parts, rows, width = data_ref.shape
    pair = rows // PAIR_GROUP
    frames = pair // 2

    @pl.when(step == 0)
    def _():
        total_ref[...] = jnp.zeros_like(total_ref)

    pieces = [
        data_ref[:, i * pair : (i + 1) * pair, :].reshape(parts * pair, width) for i in range(PAIR_GROUP)
    ]
    data = jnp.concatenate(pieces, axis=1)
    total_ref[...] += lax.dot_general(data, data, (((1,), (1,)), ((), ())), preferred_element_type=jnp.float32)

    @pl.when(step == pl.num_programs(0) - 1)
    def _():
        total = total_ref[...].reshape(parts, 2, frames, parts * pair)
        result = None
        for parity in range(2):
            rows = total[:, parity].reshape(parts * frames, parts * pair)
            selector = jnp.where(spread_selector(parity, frames), 1.0, 0.0)
            term = jnp.dot(rows, selector, precision=highest, preferred_element_type=jnp.float32)
            result = term if result is None else result + term
        out_ref[...] = result


def covariance_part(columns):
    parts, rows, width = columns.shape
    block = PAIR_GROUP * 2 * rows // ROWS_DEV
    return pl.pallas_call(
        covariance_kernel,
        grid=(rows // block,),
        in_specs=[pl.BlockSpec((parts, block, width), lambda i: (0, i, 0))],
        out_specs=pl.BlockSpec((FRAMES, FRAMES), lambda i: (0, 0)),
        out_shape=pltpu.VMEM((FRAMES, FRAMES), jnp.float32),
        scratch_shapes=[pltpu.VMEM((2 * FRAMES, 2 * FRAMES), jnp.float32)],
        name="covariance",
    )(columns)


def loading_kernel(weights_ref, data_ref, out_ref, matrix_ref, turn_ref):
    rank, height, width = out_ref.shape
    parts, rows, _ = data_ref.shape
    frames = rows // height
    pair = 2 * frames

    @pl.when(pl.program_id(0) == 0)
    def _():
        weights = weights_ref[...].astype(jnp.bfloat16)
        for parity in range(2):
            selector = jnp.where(spread_selector(parity, frames), 1.0, 0.0).astype(jnp.bfloat16)
            spread = lax.dot_general(
                weights, selector, (((1,), (1,)), ((), ())), preferred_element_type=jnp.float32
            )
            matrix_ref[parity * rank : (parity + 1) * rank, :] = spread.astype(jnp.bfloat16)

    matrix = matrix_ref[...]
    for i in range(height // 2):
        data = data_ref[:, i * pair : (i + 1) * pair, :].reshape(parts * pair, width)
        result = dot_bf16(matrix, data)
        for parity in range(2):
            for half in range(width // 128):
                lanes = slice(half * 128, (half + 1) * 128)
                turn_ref[half, pl.ds(2 * i + parity, rank, stride=height), :] = result[
                    parity * rank : (parity + 1) * rank, lanes
                ]
    for half in range(width // 128):
        lanes = slice(half * 128, (half + 1) * 128)
        out_ref[:, :, lanes] = turn_ref[half].reshape(rank, height, 128).astype(jnp.bfloat16)


def loading_rows(weights, columns):
    parts, rows, width = columns.shape
    height = LOADING_ROWS
    return pl.pallas_call(
        loading_kernel,
        grid=(ROWS_DEV // height,),
        in_specs=[vmem, pl.BlockSpec((parts, height * (rows // ROWS_DEV), width), lambda i: (0, i, 0))],
        out_specs=pl.BlockSpec((RANK, height, width), lambda i: (0, i, 0)),
        out_shape=jax.ShapeDtypeStruct((RANK, ROWS_DEV, width), jnp.bfloat16),
        scratch_shapes=[
            pltpu.VMEM((2 * RANK, 2 * FRAMES), jnp.bfloat16),
            pltpu.VMEM((width // 128, RANK * height, 128), jnp.float32),
        ],
        name="loadings",
    )(*near(weights), columns)


def split_in_three(value):
    high = value.astype(jnp.bfloat16).astype(jnp.float32)
    rest = value - high
    middle = rest.astype(jnp.bfloat16).astype(jnp.float32)
    return high, middle, rest - middle


def exact_dot(left, right):
    rows = left.shape[0]
    high, middle, low = [part.astype(jnp.bfloat16) for part in split_in_three(left)]
    right_high, right_middle, right_low = [part.astype(jnp.bfloat16) for part in split_in_three(right)]
    first = dot_bf16(jnp.concatenate([high, middle, low], axis=0), right_high)
    second = dot_bf16(jnp.concatenate([high, middle], axis=0), right_middle)
    third = dot_bf16(high, right_low)
    small = first[2 * rows :] + (second[rows:] + third)
    return first[:rows] + (first[rows : 2 * rows] + second[:rows] + small)


def solve_with_factors(systems):
    size, width = systems[0].shape
    lanes = 128
    sub = lax.broadcasted_iota(jnp.int32, (BLOCK, lanes), 0)

    def wide(value):
        return jnp.concatenate([value] * (width // lanes), axis=1)

    def spread_row(value, j):
        return jnp.broadcast_to(value[j : j + 1], value.shape)

    def spread_columns(value, start):
        return [
            jnp.broadcast_to(value[:, start + k : start + k + 1], (BLOCK, lanes)) for k in range(BLOCK)
        ]

    total = range(len(systems))
    panel = [system[:BLOCK] for system in systems]
    rest = [system[BLOCK:] for system in systems]
    done = [[] for _ in total]
    for start in range(0, size, BLOCK):
        after = start + BLOCK
        last = after == size
        columns = [spread_columns(panel[i], start) for i in total]
        if not last:
            following = [rest[i][:BLOCK] for i in total]
            next_columns = [spread_columns(following[i], start) for i in total]
        scale = [None for _ in total]
        for j in range(BLOCK):
            for i in total:
                own = columns[i]
                root = lax.rsqrt(spread_row(own[j], j))
                inverse = root * root
                for k in range(j + 1, BLOCK):
                    ratio = spread_row(own[j], k) * inverse
                    own[k] = own[k] - own[j] * ratio
                    if not last:
                        next_columns[i][k] = next_columns[i][k] - next_columns[i][j] * ratio
                pivot_row = spread_row(panel[i], j) * wide(inverse)
                if j < BLOCK - 1:
                    panel[i] = panel[i] - wide(jnp.where(sub > j, own[j], 0.0)) * pivot_row
                if not last:
                    following[i] = following[i] - wide(next_columns[i][j]) * pivot_row
                scale[i] = root if scale[i] is None else jnp.where(sub == j, root, scale[i])
        for i in total:
            solved = panel[i] * wide(scale[i])
            done[i].append(solved[:, lanes:])
            if last:
                continue
            panel[i] = following[i]
            if after + BLOCK < size:
                high, middle, low = split_in_three(solved)
                left = jnp.concatenate(
                    [part[:, :lanes] for part in (high, high, middle, high, middle, low)], axis=0
                )
                left = left.T[after + BLOCK : size].astype(jnp.bfloat16)
                right = jnp.concatenate([high, middle, high, low, middle, high], axis=0)
                rest[i] = rest[i][BLOCK:] - dot_bf16(left, right.astype(jnp.bfloat16))
    return [jnp.concatenate(rows, axis=0) for rows in done]


def store_rows(rows_ref, rows):
    if len(rows_ref.shape) == 2:
        rows_ref[...] = rows
    else:
        for copy in range(rows_ref.shape[0]):
            rows_ref[copy] = rows


def rows_and_weights(copies):
    shape = (RANK, FRAMES) if copies == 1 else (copies, RANK, FRAMES)
    return dict(
        out_specs=[vmem, vmem],
        out_shape=[pltpu.VMEM(shape, jnp.float32), pltpu.VMEM((RANK, FRAMES), jnp.float32)],
    )


def basis_kernel(covariance_ref, test_ref, rows_ref, weights_ref):
    covariance = covariance_ref[...] * (1.0 / (ROWS_DEV * COLS))
    sketch = exact_dot(covariance, test_ref[...])
    image = exact_dot(covariance, sketch)
    turned = sketch.T[:RANK]
    system = exact_dot(turned, jnp.concatenate([image, covariance], axis=1))
    (solved,) = solve_with_factors([jnp.concatenate([system, turned], axis=1)])
    store_rows(rows_ref, solved[:, :FRAMES])
    weights_ref[...] = solved[:, FRAMES:]


def tile_basis(covariance, test_matrix, copies=1):
    return pl.pallas_call(
        basis_kernel, in_specs=[vmem, vmem], name="basis", **rows_and_weights(copies)
    )(*near(covariance, test_matrix))


def merge_nodes(stacks, placed, probe):
    systems = []
    for stacked, weights in zip(stacks, placed):
        sketch = exact_dot(stacked, exact_dot(stacked.T, probe))
        systems.append(exact_dot(sketch.T[:RANK], jnp.concatenate([sketch, stacked, weights], axis=1)))
    solved = solve_with_factors(systems)
    rows = [result[:, :FRAMES] * reduction_multiplier for result in solved]
    weights = sum([result[:, FRAMES:] for result in solved[1:]], solved[0][:, FRAMES:])
    return rows, weights * growth_multiplier


def place(weights, first, second):
    return jnp.concatenate([jnp.where(first, weights, 0.0), jnp.where(second, weights, 0.0)], axis=0)


def merge_kernel(place_ref, own_ref, partner_ref, weights_ref, probe_ref, rows_ref, new_weights_ref):
    is_first = place_ref[0] == 0
    own = own_ref[...]
    partner = partner_ref[...]
    stacked = jnp.concatenate([jnp.where(is_first, own, partner), jnp.where(is_first, partner, own)], axis=0)
    placed = place(weights_ref[...], is_first, jnp.logical_not(is_first))
    (rows,), weights = merge_nodes([stacked], [placed], probe_ref[...])
    store_rows(rows_ref, rows)
    new_weights_ref[...] = weights


def merge(place_in, own, partner, weights, probe, copies=1):
    return pl.pallas_call(
        merge_kernel, in_specs=[smem, vmem, vmem, vmem, vmem], name="merge", **rows_and_weights(copies)
    )(place_in, *near(own, partner, weights, probe))


def merge_four_kernel(place_ref, rows_in_ref, weights_ref, probe_ref, rows_ref, new_weights_ref):
    spot = place_ref[0]
    probe = probe_ref[...]
    weights = weights_ref[...]
    stacks = [rows_in_ref[2 * m : 2 * m + 2].reshape(2 * RANK, FRAMES) for m in range(2)]
    placed = [place(weights, spot == 2 * m, spot == 2 * m + 1) for m in range(2)]
    rows, weights = merge_nodes(stacks, placed, probe)
    (rows,), weights = merge_nodes([jnp.concatenate(rows, axis=0)], [place(weights, spot < 2, spot >= 2)], probe)
    store_rows(rows_ref, rows)
    new_weights_ref[...] = weights


def merge_four(place_in, gathered, weights, probe, copies=1):
    return pl.pallas_call(
        merge_four_kernel, in_specs=[smem, vmem, vmem, vmem], name="merge_four", **rows_and_weights(copies)
    )(place_in, *near(gathered, weights, probe))


def sum_over_tm(partial):
    parts = lax.axis_size("tm")
    height = partial.shape[0] // parts
    pieces = lax.all_to_all(partial.reshape(parts, height, -1), "tm", 0, 0, tiled=True)
    own = jnp.sum(pieces, axis=0, keepdims=True)
    whole = lax.all_to_all(jnp.broadcast_to(own, pieces.shape), "tm", 0, 0, tiled=True)
    return whole.reshape(partial.shape)


def body(movie_frames, depth_index, depth_width, temporal_test_matrix, merge_probe):
    frames = movie_frames.shape[0]
    parts = lax.axis_size("tm")
    count = lax.axis_size("pix")
    forward = [(i, i + 1) for i in range(count - 1)]
    backward = [(target, source) for source, target in forward]
    low = lax.ppermute(movie_frames[:, ROWS_DEV - HW :].reshape(frames * HW, COLS), "pix", forward)
    high = lax.ppermute(movie_frames[:, :HW].reshape(frames * HW, COLS), "pix", backward)
    matrices = smoothing_matrices(row_weights(depth_index, depth_width), frames)
    smoothed = smooth_tile(movie_frames, low, high, matrices, parts)
    columns = lax.all_to_all(smoothed, "tm", 0, 0, tiled=True)
    covariance = sum_over_tm(covariance_part(columns))
    spare = FRAMES - RANK
    test_matrix = jnp.pad(temporal_test_matrix, ((0, 0), (0, spare)))
    probe = jnp.pad(merge_probe, ((0, 0), (0, spare)))
    position = lax.axis_index("pix").astype(jnp.int32)
    levels = count.bit_length() - 1
    sizes = []
    while sum(sizes) < levels:
        sizes.append(2 if levels - sum(sizes) == 2 else 1)
    copies = [4 if size == 2 else 1 for size in sizes[1:]] + [1]
    rows, weights = tile_basis(covariance, test_matrix, 4 if sizes[0] == 2 else 1)
    level = 0
    for size, next_copies in zip(sizes, copies):
        spot = (position >> level & (2**size - 1)).reshape(1)
        if size == 2:
            step = 1 << level
            groups = [
                [base + k * step for k in range(4)] for base in range(count) if not base & (3 * step)
            ]
            gathered = lax.all_to_all(rows, "pix", 0, 0, tiled=True, axis_index_groups=groups)
            rows, weights = merge_four(spot, gathered, weights, probe, next_copies)
        else:
            pairs = [(source, source ^ (1 << level)) for source in range(count)]
            partner = lax.ppermute(rows, "pix", pairs)
            rows, weights = merge(spot, rows, partner, weights, probe, next_copies)
        level += size
    loadings = loading_rows(weights, columns)
    own_times = lax.dynamic_slice_in_dim(rows, lax.axis_index("tm") * frames, frames, 1)
    return (own_times, loadings)


def solution(mesh):
    in_specs = (P("tm", "pix", None), P("pix"), P(), P(), P())
    out_specs = (P(None, "tm"), P(None, "pix", "tm"))
    return jax.shard_map(body, mesh=mesh, in_specs=in_specs, out_specs=out_specs, check_vma=False)
```

```python
import math

import jax
import jax.numpy as jnp
from jax import lax
from jax.experimental import pallas as pl
from jax.experimental.pallas import tpu as pltpu
from jax.sharding import PartitionSpec as P

ROWS_DEV = 32
COLS = 4096
FRAMES = 128
RANK = 96
HW = 4
NDEPTH = 6
BLOCK = 8
SMOOTH_GROUP = 4
PAIR_GROUP = 8
LOADING_ROWS = 16

highest = lax.Precision.HIGHEST
reduction_multiplier = math.sqrt(0.5)
growth_multiplier = math.sqrt(2.0)
vmem = pl.BlockSpec(memory_space=pltpu.VMEM)
smem = pl.BlockSpec(memory_space=pltpu.SMEM)


def near(*values):
    return [pltpu.with_memory_space_constraint(value, pltpu.VMEM) for value in values]


def taps_table(depth_width):
    offsets = jnp.arange(-HW, HW + 1).astype(jnp.float32)
    kernel_raw = jnp.exp(-offsets[None, :] ** 2 / (2.0 * depth_width[:, None] ** 2))
    return kernel_raw / jnp.sum(kernel_raw, axis=1, keepdims=True)


def row_weights(row_depth, depth_width):
    classes = jnp.arange(NDEPTH)
    onehot = (row_depth[:, None] == classes[None, :]).astype(jnp.float32)
    return jnp.dot(onehot, taps_table(depth_width), precision=highest)


def split_bf16(value):
    high = lax.reduce_precision(value, exponent_bits=8, mantissa_bits=7)
    return high.astype(jnp.bfloat16), (value - high).astype(jnp.bfloat16)


def smoothing_matrices(weights, frames):
    def matrix(spread, out_row, out_frame, in_row, in_frame):
        tap = jnp.where(in_frame[None, :] == out_frame[:, None], in_row[None, :] - out_row[:, None], -1)
        total = jnp.zeros(tap.shape, jnp.float32)
        for offset in range(2 * HW + 1):
            total = total + jnp.where(tap == offset, spread[:, offset : offset + 1], 0.0)
        high, low = split_bf16(total)
        return jnp.concatenate([high, low], axis=0)

    index = jnp.arange(frames * ROWS_DEV)
    own = matrix(
        jnp.repeat(weights, frames, axis=0),
        index // frames,
        index % frames,
        index % ROWS_DEV + HW,
        index // ROWS_DEV,
    )
    index = jnp.arange(frames * HW)
    edge_rows = index // frames
    sides = [
        matrix(
            jnp.repeat(weights[first : first + HW], frames, axis=0),
            edge_rows + first,
            index % frames,
            index % HW + (first + 2 * HW if first else 0),
            index // HW,
        )
        for first in (0, ROWS_DEV - HW)
    ]
    return own, jnp.concatenate(sides, axis=0)


def dot_bf16(left, right):
    return lax.dot_general(left, right, (((1,), (0,)), ((), ())), preferred_element_type=jnp.float32)


def smooth_kernel(movie_ref, own_ref, out_ref, edges_ref):
    frames, rows, _ = movie_ref.shape
    count, out_rows, width = out_ref.shape
    edge = edges_ref.shape[1] // 2
    start = pl.program_id(0) * count
    own = own_ref[...]
    for part in range(count):
        movie = movie_ref[:, :, part * width : (part + 1) * width].reshape(frames * rows, width)
        both = dot_bf16(own, movie)
        total = both[:out_rows] + both[out_rows:]
        out_ref[part] = total.astype(jnp.bfloat16)
        edges_ref[start + part, :edge] = total[:edge]
        edges_ref[start + part, edge:] = total[out_rows - edge :]


def edge_kernel(_, edges_ref, low_ref, high_ref, matrix_ref, out_ref):
    count, edge, width = out_ref.shape
    side = pl.program_id(0)
    rows = pl.ds(pl.multiple_of(side * edge, edge), edge)
    matrix = matrix_ref[pl.ds(pl.multiple_of(side * 2 * edge, 2 * edge), 2 * edge), :]
    for part in range(count):
        lanes = slice(part * width, (part + 1) * width)
        halo = jnp.where(side == 0, low_ref[:, lanes], high_ref[:, lanes])
        both = dot_bf16(matrix, halo)
        out_ref[part] = (edges_ref[part, rows, :] + (both[:edge] + both[edge:])).astype(jnp.bfloat16)


def smooth_tile(movie, low, high, matrices, parts):
    frames = movie.shape[0]
    width = COLS // parts
    rows = frames * ROWS_DEV
    edge = frames * HW
    group = SMOOTH_GROUP
    own, sides = matrices
    shape = jax.ShapeDtypeStruct((parts, rows, width), jnp.bfloat16)
    smoothed, edges = pl.pallas_call(
        smooth_kernel,
        grid=(parts // group,),
        in_specs=[pl.BlockSpec((frames, ROWS_DEV, group * width), lambda i: (0, 0, i)), vmem],
        out_specs=[pl.BlockSpec((group, rows, width), lambda i: (i, 0, 0)), vmem],
        out_shape=[shape, pltpu.VMEM((parts, 2 * edge, width), jnp.float32)],
        name="smooth",
    )(movie, *near(own))
    return pl.pallas_call(
        edge_kernel,
        grid=(2,),
        in_specs=[pl.BlockSpec(memory_space=pl.ANY), vmem, vmem, vmem, vmem],
        out_specs=pl.BlockSpec((parts, edge, width), lambda i: (0, i * (rows // edge - 1), 0)),
        out_shape=shape,
        input_output_aliases={0: 0},
        name="edges",
    )(smoothed, *near(edges, low, high, sides))


def spread_selector(parity, frames):
    row = lax.broadcasted_iota(jnp.int32, (2 * FRAMES, FRAMES), 0)
    col = lax.broadcasted_iota(jnp.int32, (2 * FRAMES, FRAMES), 1)
    wanted = col // frames * (2 * frames) + parity * frames + col % frames
    return row == wanted


def covariance_kernel(data_ref, out_ref, total_ref):
    step = pl.program_id(0)
    parts, rows, width = data_ref.shape
    pair = rows // PAIR_GROUP
    frames = pair // 2

    @pl.when(step == 0)
    def _():
        total_ref[...] = jnp.zeros_like(total_ref)

    pieces = [
        data_ref[:, i * pair : (i + 1) * pair, :].reshape(parts * pair, width) for i in range(PAIR_GROUP)
    ]
    data = jnp.concatenate(pieces, axis=1)
    total_ref[...] += lax.dot_general(data, data, (((1,), (1,)), ((), ())), preferred_element_type=jnp.float32)

    @pl.when(step == pl.num_programs(0) - 1)
    def _():
        total = total_ref[...].reshape(parts, 2, frames, parts * pair)
        result = None
        for parity in range(2):
            rows = total[:, parity].reshape(parts * frames, parts * pair)
            selector = jnp.where(spread_selector(parity, frames), 1.0, 0.0)
            term = jnp.dot(rows, selector, precision=highest, preferred_element_type=jnp.float32)
            result = term if result is None else result + term
        out_ref[...] = result


def covariance_part(columns):
    parts, rows, width = columns.shape
    block = PAIR_GROUP * 2 * rows // ROWS_DEV
    return pl.pallas_call(
        covariance_kernel,
        grid=(rows // block,),
        in_specs=[pl.BlockSpec((parts, block, width), lambda i: (0, i, 0))],
        out_specs=pl.BlockSpec((FRAMES, FRAMES), lambda i: (0, 0)),
        out_shape=pltpu.VMEM((FRAMES, FRAMES), jnp.float32),
        scratch_shapes=[pltpu.VMEM((2 * FRAMES, 2 * FRAMES), jnp.float32)],
        name="covariance",
    )(columns)


def loading_kernel(weights_ref, data_ref, out_ref, matrix_ref, turn_ref):
    rank, height, width = out_ref.shape
    parts, rows, _ = data_ref.shape
    frames = rows // height
    pair = 2 * frames

    @pl.when(pl.program_id(0) == 0)
    def _():
        weights = weights_ref[...].astype(jnp.bfloat16)
        for parity in range(2):
            selector = jnp.where(spread_selector(parity, frames), 1.0, 0.0).astype(jnp.bfloat16)
            spread = lax.dot_general(
                weights, selector, (((1,), (1,)), ((), ())), preferred_element_type=jnp.float32
            )
            matrix_ref[parity * rank : (parity + 1) * rank, :] = spread.astype(jnp.bfloat16)

    matrix = matrix_ref[...]
    for i in range(height // 2):
        data = data_ref[:, i * pair : (i + 1) * pair, :].reshape(parts * pair, width)
        result = dot_bf16(matrix, data)
        for parity in range(2):
            for half in range(width // 128):
                lanes = slice(half * 128, (half + 1) * 128)
                turn_ref[half, pl.ds(2 * i + parity, rank, stride=height), :] = result[
                    parity * rank : (parity + 1) * rank, lanes
                ]
    for half in range(width // 128):
        lanes = slice(half * 128, (half + 1) * 128)
        out_ref[:, :, lanes] = turn_ref[half].reshape(rank, height, 128).astype(jnp.bfloat16)


def loading_rows(weights, columns):
    parts, rows, width = columns.shape
    height = LOADING_ROWS
    return pl.pallas_call(
        loading_kernel,
        grid=(ROWS_DEV // height,),
        in_specs=[vmem, pl.BlockSpec((parts, height * (rows // ROWS_DEV), width), lambda i: (0, i, 0))],
        out_specs=pl.BlockSpec((RANK, height, width), lambda i: (0, i, 0)),
        out_shape=jax.ShapeDtypeStruct((RANK, ROWS_DEV, width), jnp.bfloat16),
        scratch_shapes=[
            pltpu.VMEM((2 * RANK, 2 * FRAMES), jnp.bfloat16),
            pltpu.VMEM((width // 128, RANK * height, 128), jnp.float32),
        ],
        name="loadings",
    )(*near(weights), columns)


def split_in_three(value):
    high = value.astype(jnp.bfloat16).astype(jnp.float32)
    rest = value - high
    middle = rest.astype(jnp.bfloat16).astype(jnp.float32)
    return high, middle, rest - middle


def exact_dot(left, right):
    rows = left.shape[0]
    high, middle, low = [part.astype(jnp.bfloat16) for part in split_in_three(left)]
    right_high, right_middle, right_low = [part.astype(jnp.bfloat16) for part in split_in_three(right)]
    first = dot_bf16(jnp.concatenate([high, middle, low], axis=0), right_high)
    second = dot_bf16(jnp.concatenate([high, middle], axis=0), right_middle)
    third = dot_bf16(high, right_low)
    small = first[2 * rows :] + (second[rows:] + third)
    return first[:rows] + (first[rows : 2 * rows] + second[:rows] + small)


def solve_with_factors(systems):
    size, width = systems[0].shape
    lanes = 128
    sub = lax.broadcasted_iota(jnp.int32, (BLOCK, lanes), 0)

    def wide(value):
        return jnp.concatenate([value] * (width // lanes), axis=1)

    def spread_row(value, j):
        return jnp.broadcast_to(value[j : j + 1], value.shape)

    def spread_columns(value, start):
        return [
            jnp.broadcast_to(value[:, start + k : start + k + 1], (BLOCK, lanes)) for k in range(BLOCK)
        ]

    total = range(len(systems))
    panel = [system[:BLOCK] for system in systems]
    rest = [system[BLOCK:] for system in systems]
    done = [[] for _ in total]
    for start in range(0, size, BLOCK):
        after = start + BLOCK
        last = after == size
        columns = [spread_columns(panel[i], start) for i in total]
        if not last:
            following = [rest[i][:BLOCK] for i in total]
            next_columns = [spread_columns(following[i], start) for i in total]
        scale = [None for _ in total]
        for j in range(BLOCK):
            for i in total:
                own = columns[i]
                root = lax.rsqrt(spread_row(own[j], j))
                inverse = root * root
                for k in range(j + 1, BLOCK):
                    ratio = spread_row(own[j], k) * inverse
                    own[k] = own[k] - own[j] * ratio
                    if not last:
                        next_columns[i][k] = next_columns[i][k] - next_columns[i][j] * ratio
                pivot_row = spread_row(panel[i], j) * wide(inverse)
                if j < BLOCK - 1:
                    panel[i] = panel[i] - wide(jnp.where(sub > j, own[j], 0.0)) * pivot_row
                if not last:
                    following[i] = following[i] - wide(next_columns[i][j]) * pivot_row
                scale[i] = root if scale[i] is None else jnp.where(sub == j, root, scale[i])
        for i in total:
            solved = panel[i] * wide(scale[i])
            done[i].append(solved[:, lanes:])
            if last:
                continue
            panel[i] = following[i]
            if after + BLOCK < size:
                high, middle, low = split_in_three(solved)
                left = jnp.concatenate(
                    [part[:, :lanes] for part in (high, high, middle, high, middle, low)], axis=0
                )
                left = left.T[after + BLOCK : size].astype(jnp.bfloat16)
                right = jnp.concatenate([high, middle, high, low, middle, high], axis=0)
                rest[i] = rest[i][BLOCK:] - dot_bf16(left, right.astype(jnp.bfloat16))
    return [jnp.concatenate(rows, axis=0) for rows in done]


def store_rows(rows_ref, rows):
    if len(rows_ref.shape) == 2:
        rows_ref[...] = rows
    else:
        for copy in range(rows_ref.shape[0]):
            rows_ref[copy] = rows


def rows_and_weights(copies):
    shape = (RANK, FRAMES) if copies == 1 else (copies, RANK, FRAMES)
    return dict(
        out_specs=[vmem, vmem],
        out_shape=[pltpu.VMEM(shape, jnp.float32), pltpu.VMEM((RANK, FRAMES), jnp.float32)],
    )


def basis_kernel(covariance_ref, test_ref, rows_ref, weights_ref):
    covariance = covariance_ref[...] * (1.0 / (ROWS_DEV * COLS))
    largest = jnp.max(jnp.max(covariance, axis=0, keepdims=True), axis=1, keepdims=True)
    root = lax.rsqrt(largest)
    covariance = covariance * root * root
    sketch = exact_dot(covariance, test_ref[...])
    image = exact_dot(covariance, sketch)
    turned = sketch.T[:RANK]
    system = exact_dot(turned, jnp.concatenate([image, covariance], axis=1))
    (solved,) = solve_with_factors([jnp.concatenate([system, turned], axis=1)])
    store_rows(rows_ref, solved[:, :FRAMES] * (largest * root))
    weights_ref[...] = solved[:, FRAMES:] * root


def tile_basis(covariance, test_matrix, copies=1):
    return pl.pallas_call(
        basis_kernel, in_specs=[vmem, vmem], name="basis", **rows_and_weights(copies)
    )(*near(covariance, test_matrix))


def merge_nodes(stacks, placed, probe):
    systems = []
    for stacked, weights in zip(stacks, placed):
        sketch = exact_dot(stacked, exact_dot(stacked.T, probe))
        systems.append(exact_dot(sketch.T[:RANK], jnp.concatenate([sketch, stacked, weights], axis=1)))
    solved = solve_with_factors(systems)
    rows = [result[:, :FRAMES] * reduction_multiplier for result in solved]
    weights = sum([result[:, FRAMES:] for result in solved[1:]], solved[0][:, FRAMES:])
    return rows, weights * growth_multiplier


def place(weights, first, second):
    return jnp.concatenate([jnp.where(first, weights, 0.0), jnp.where(second, weights, 0.0)], axis=0)


def merge_kernel(place_ref, own_ref, partner_ref, weights_ref, probe_ref, rows_ref, new_weights_ref):
    is_first = place_ref[0] == 0
    own = own_ref[...]
    partner = partner_ref[...]
    stacked = jnp.concatenate([jnp.where(is_first, own, partner), jnp.where(is_first, partner, own)], axis=0)
    placed = place(weights_ref[...], is_first, jnp.logical_not(is_first))
    (rows,), weights = merge_nodes([stacked], [placed], probe_ref[...])
    store_rows(rows_ref, rows)
    new_weights_ref[...] = weights


def merge(place_in, own, partner, weights, probe, copies=1):
    return pl.pallas_call(
        merge_kernel, in_specs=[smem, vmem, vmem, vmem, vmem], name="merge", **rows_and_weights(copies)
    )(place_in, *near(own, partner, weights, probe))


def merge_four_kernel(
    place_ref, rows_in_ref, weights_ref, probe_ref, times_ref, new_weights_ref, turned_ref
):
    spot = place_ref[0]
    frames = times_ref.shape[0]
    probe = probe_ref[...]
    weights = weights_ref[...]
    stacks = [rows_in_ref[2 * m : 2 * m + 2].reshape(2 * RANK, FRAMES) for m in range(2)]
    placed = [place(weights, spot == 2 * m, spot == 2 * m + 1) for m in range(2)]
    rows, weights = merge_nodes(stacks, placed, probe)
    (rows,), weights = merge_nodes([jnp.concatenate(rows, axis=0)], [place(weights, spot < 2, spot >= 2)], probe)
    new_weights_ref[...] = weights
    turned_ref[...] = rows.T
    times_ref[...] = turned_ref[pl.ds(pl.multiple_of(place_ref[1] * frames, frames), frames), :]


def merge_four(place_in, gathered, weights, probe, frames):
    return pl.pallas_call(
        merge_four_kernel,
        in_specs=[smem, vmem, vmem, vmem],
        out_specs=[vmem, vmem],
        out_shape=[
            jax.ShapeDtypeStruct((frames, RANK), jnp.float32),
            pltpu.VMEM((RANK, FRAMES), jnp.float32),
        ],
        scratch_shapes=[pltpu.VMEM((FRAMES, RANK), jnp.float32)],
        name="merge_four",
    )(place_in, *near(gathered, weights, probe))


def sum_over_tm(partial):
    parts = lax.axis_size("tm")
    height = partial.shape[0] // parts
    pieces = lax.all_to_all(partial.reshape(parts, height, -1), "tm", 0, 0, tiled=True)
    own = jnp.sum(pieces, axis=0, keepdims=True)
    whole = lax.all_to_all(jnp.broadcast_to(own, pieces.shape), "tm", 0, 0, tiled=True)
    return whole.reshape(partial.shape)


def body(movie_frames, depth_index, depth_width, temporal_test_matrix, merge_probe):
    frames = movie_frames.shape[0]
    parts = lax.axis_size("tm")
    count = lax.axis_size("pix")
    forward = [(i, i + 1) for i in range(count - 1)]
    backward = [(target, source) for source, target in forward]
    low = lax.ppermute(movie_frames[:, ROWS_DEV - HW :].reshape(frames * HW, COLS), "pix", forward)
    high = lax.ppermute(movie_frames[:, :HW].reshape(frames * HW, COLS), "pix", backward)
    matrices = smoothing_matrices(row_weights(depth_index, depth_width), frames)
    smoothed = smooth_tile(movie_frames, low, high, matrices, parts)
    columns = lax.all_to_all(smoothed, "tm", 0, 0, tiled=True)
    covariance = sum_over_tm(covariance_part(columns))
    spare = FRAMES - RANK
    test_matrix = jnp.pad(temporal_test_matrix, ((0, 0), (0, spare)))
    probe = jnp.pad(merge_probe, ((0, 0), (0, spare)))
    position = lax.axis_index("pix").astype(jnp.int32)
    levels = count.bit_length() - 1
    rows, weights = tile_basis(covariance, test_matrix)
    for level in range(levels - 2):
        pairs = [(source, source ^ (1 << level)) for source in range(count)]
        partner = lax.ppermute(rows, "pix", pairs)
        spot = (position >> level & 1).reshape(1)
        rows, weights = merge(spot, rows, partner, weights, probe, 4 if level == levels - 3 else 1)
    step = count // 4
    groups = [[base + k * step for k in range(4)] for base in range(step)]
    gathered = lax.all_to_all(rows, "pix", 0, 0, tiled=True, axis_index_groups=groups)
    spot = jnp.stack([position // step, lax.axis_index("tm").astype(jnp.int32)])
    own_times, weights = merge_four(spot, gathered, weights, probe, frames)
    loadings = loading_rows(weights, columns)
    return (own_times.T, loadings)


def solution(mesh):
    in_specs = (P("tm", "pix", None), P("pix"), P(), P(), P())
    out_specs = (P(None, "tm"), P(None, "pix", "tm"))
    return jax.shard_map(body, mesh=mesh, in_specs=in_specs, out_specs=out_specs, check_vma=False)
```

```python
import math

import jax
import jax.numpy as jnp
from jax import lax
from jax.experimental import pallas as pl
from jax.experimental.pallas import tpu as pltpu
from jax.sharding import PartitionSpec as P

ROWS_DEV = 32
COLS = 4096
FRAMES = 128
RANK = 96
HW = 4
NDEPTH = 6
BLOCK = 8
SMOOTH_GROUP = 4
PAIR_GROUP = 8
LOADING_ROWS = 16

highest = lax.Precision.HIGHEST
reduction_multiplier = math.sqrt(0.5)
growth_multiplier = math.sqrt(2.0)
vmem = pl.BlockSpec(memory_space=pltpu.VMEM)
smem = pl.BlockSpec(memory_space=pltpu.SMEM)


def near(*values):
    return [pltpu.with_memory_space_constraint(value, pltpu.VMEM) for value in values]


def taps_table(depth_width):
    offsets = jnp.arange(-HW, HW + 1).astype(jnp.float32)
    kernel_raw = jnp.exp(-offsets[None, :] ** 2 / (2.0 * depth_width[:, None] ** 2))
    return kernel_raw / jnp.sum(kernel_raw, axis=1, keepdims=True)


def row_weights(row_depth, depth_width):
    classes = jnp.arange(NDEPTH)
    onehot = (row_depth[:, None] == classes[None, :]).astype(jnp.float32)
    return jnp.dot(onehot, taps_table(depth_width), precision=highest)


def split_bf16(value):
    high = lax.reduce_precision(value, exponent_bits=8, mantissa_bits=7)
    return high.astype(jnp.bfloat16), (value - high).astype(jnp.bfloat16)


def smoothing_matrices(weights, frames):
    def matrix(spread, out_row, out_frame, in_row, in_frame):
        tap = jnp.where(in_frame[None, :] == out_frame[:, None], in_row[None, :] - out_row[:, None], -1)
        total = jnp.zeros(tap.shape, jnp.float32)
        for offset in range(2 * HW + 1):
            total = total + jnp.where(tap == offset, spread[:, offset : offset + 1], 0.0)
        high, low = split_bf16(total)
        return jnp.concatenate([high, low], axis=0)

    index = jnp.arange(frames * ROWS_DEV)
    own = matrix(
        jnp.repeat(weights, frames, axis=0),
        index // frames,
        index % frames,
        index % ROWS_DEV + HW,
        index // ROWS_DEV,
    )
    index = jnp.arange(frames * HW)
    edge_rows = index // frames
    sides = [
        matrix(
            jnp.repeat(weights[first : first + HW], frames, axis=0),
            edge_rows + first,
            index % frames,
            index % HW + (first + 2 * HW if first else 0),
            index // HW,
        )
        for first in (0, ROWS_DEV - HW)
    ]
    return own, jnp.concatenate(sides, axis=0)


def dot_bf16(left, right):
    return lax.dot_general(left, right, (((1,), (0,)), ((), ())), preferred_element_type=jnp.float32)


def smooth_kernel(movie_ref, own_ref, out_ref, edges_ref):
    frames, rows, _ = movie_ref.shape
    count, out_rows, width = out_ref.shape
    edge = edges_ref.shape[1] // 2
    start = pl.program_id(0) * count
    own = own_ref[...]
    for part in range(count):
        movie = movie_ref[:, :, part * width : (part + 1) * width].reshape(frames * rows, width)
        both = dot_bf16(own, movie)
        total = both[:out_rows] + both[out_rows:]
        out_ref[part] = total.astype(jnp.bfloat16)
        edges_ref[start + part, :edge] = total[:edge]
        edges_ref[start + part, edge:] = total[out_rows - edge :]


def edge_kernel(_, edges_ref, low_ref, high_ref, matrix_ref, out_ref):
    count, edge, width = out_ref.shape
    side = pl.program_id(0)
    rows = pl.ds(pl.multiple_of(side * edge, edge), edge)
    matrix = matrix_ref[pl.ds(pl.multiple_of(side * 2 * edge, 2 * edge), 2 * edge), :]
    for part in range(count):
        lanes = slice(part * width, (part + 1) * width)
        halo = jnp.where(side == 0, low_ref[:, lanes], high_ref[:, lanes])
        both = dot_bf16(matrix, halo)
        out_ref[part] = (edges_ref[part, rows, :] + (both[:edge] + both[edge:])).astype(jnp.bfloat16)


def smooth_tile(movie, low, high, matrices, parts):
    frames = movie.shape[0]
    width = COLS // parts
    rows = frames * ROWS_DEV
    edge = frames * HW
    group = SMOOTH_GROUP
    own, sides = matrices
    shape = jax.ShapeDtypeStruct((parts, rows, width), jnp.bfloat16)
    smoothed, edges = pl.pallas_call(
        smooth_kernel,
        grid=(parts // group,),
        in_specs=[pl.BlockSpec((frames, ROWS_DEV, group * width), lambda i: (0, 0, i)), vmem],
        out_specs=[pl.BlockSpec((group, rows, width), lambda i: (i, 0, 0)), vmem],
        out_shape=[shape, pltpu.VMEM((parts, 2 * edge, width), jnp.float32)],
        name="smooth",
    )(movie, *near(own))
    return pl.pallas_call(
        edge_kernel,
        grid=(2,),
        in_specs=[pl.BlockSpec(memory_space=pl.ANY), vmem, vmem, vmem, vmem],
        out_specs=pl.BlockSpec((parts, edge, width), lambda i: (0, i * (rows // edge - 1), 0)),
        out_shape=shape,
        input_output_aliases={0: 0},
        name="edges",
    )(smoothed, *near(edges, low, high, sides))


def spread_selector(parity, frames):
    row = lax.broadcasted_iota(jnp.int32, (2 * FRAMES, FRAMES), 0)
    col = lax.broadcasted_iota(jnp.int32, (2 * FRAMES, FRAMES), 1)
    wanted = col // frames * (2 * frames) + parity * frames + col % frames
    return row == wanted


def covariance_kernel(data_ref, out_ref, total_ref):
    step = pl.program_id(0)
    parts, rows, width = data_ref.shape
    pair = rows // PAIR_GROUP
    frames = pair // 2

    @pl.when(step == 0)
    def _():
        total_ref[...] = jnp.zeros_like(total_ref)

    pieces = [
        data_ref[:, i * pair : (i + 1) * pair, :].reshape(parts * pair, width) for i in range(PAIR_GROUP)
    ]
    data = jnp.concatenate(pieces, axis=1)
    total_ref[...] += lax.dot_general(data, data, (((1,), (1,)), ((), ())), preferred_element_type=jnp.float32)

    @pl.when(step == pl.num_programs(0) - 1)
    def _():
        total = total_ref[...].reshape(parts, 2, frames, parts * pair)
        result = None
        for parity in range(2):
            rows = total[:, parity].reshape(parts * frames, parts * pair)
            selector = jnp.where(spread_selector(parity, frames), 1.0, 0.0)
            term = jnp.dot(rows, selector, precision=highest, preferred_element_type=jnp.float32)
            result = term if result is None else result + term
        out_ref[...] = result


def covariance_part(columns):
    parts, rows, width = columns.shape
    block = PAIR_GROUP * 2 * rows // ROWS_DEV
    return pl.pallas_call(
        covariance_kernel,
        grid=(rows // block,),
        in_specs=[pl.BlockSpec((parts, block, width), lambda i: (0, i, 0))],
        out_specs=pl.BlockSpec((FRAMES, FRAMES), lambda i: (0, 0)),
        out_shape=pltpu.VMEM((FRAMES, FRAMES), jnp.float32),
        scratch_shapes=[pltpu.VMEM((2 * FRAMES, 2 * FRAMES), jnp.float32)],
        name="covariance",
    )(columns)


def loading_kernel(
    span_ref, rows_ref, weights_ref, data_ref, out_ref, times_ref, matrix_ref, turn_ref, times_all_ref
):
    rank, height, width = out_ref.shape
    parts, rows, _ = data_ref.shape
    frames = rows // height
    pair = 2 * frames

    @pl.when(pl.program_id(0) == 0)
    def _():
        weights = weights_ref[...].astype(jnp.bfloat16)
        for parity in range(2):
            selector = jnp.where(spread_selector(parity, frames), 1.0, 0.0).astype(jnp.bfloat16)
            spread = lax.dot_general(
                weights, selector, (((1,), (1,)), ((), ())), preferred_element_type=jnp.float32
            )
            matrix_ref[parity * rank : (parity + 1) * rank, :] = spread.astype(jnp.bfloat16)
        times_all_ref[...] = rows_ref[...].T
        times_ref[...] = times_all_ref[pl.ds(pl.multiple_of(span_ref[0] * frames, frames), frames), :]

    matrix = matrix_ref[...]
    for i in range(height // 2):
        data = data_ref[:, i * pair : (i + 1) * pair, :].reshape(parts * pair, width)
        result = dot_bf16(matrix, data)
        for parity in range(2):
            for half in range(width // 128):
                lanes = slice(half * 128, (half + 1) * 128)
                turn_ref[half, pl.ds(2 * i + parity, rank, stride=height), :] = result[
                    parity * rank : (parity + 1) * rank, lanes
                ]
    for half in range(width // 128):
        lanes = slice(half * 128, (half + 1) * 128)
        out_ref[:, :, lanes] = turn_ref[half].reshape(rank, height, 128).astype(jnp.bfloat16)


def loading_rows(span, root_rows, weights, columns):
    parts, rows, width = columns.shape
    height = LOADING_ROWS
    frames = rows // ROWS_DEV
    return pl.pallas_call(
        loading_kernel,
        grid=(ROWS_DEV // height,),
        in_specs=[smem, vmem, vmem, pl.BlockSpec((parts, height * frames, width), lambda i: (0, i, 0))],
        out_specs=[
            pl.BlockSpec((RANK, height, width), lambda i: (0, i, 0)),
            pl.BlockSpec((frames, RANK), lambda i: (0, 0)),
        ],
        out_shape=[
            jax.ShapeDtypeStruct((RANK, ROWS_DEV, width), jnp.bfloat16),
            jax.ShapeDtypeStruct((frames, RANK), jnp.float32),
        ],
        scratch_shapes=[
            pltpu.VMEM((2 * RANK, 2 * FRAMES), jnp.bfloat16),
            pltpu.VMEM((width // 128, RANK * height, 128), jnp.float32),
            pltpu.VMEM((FRAMES, RANK), jnp.float32),
        ],
        name="loadings",
    )(span, *near(root_rows, weights), columns)


def split_in_three(value):
    high = value.astype(jnp.bfloat16).astype(jnp.float32)
    rest = value - high
    middle = rest.astype(jnp.bfloat16).astype(jnp.float32)
    return high, middle, rest - middle


def exact_dot(left, right):
    rows = left.shape[0]
    high, middle, low = [part.astype(jnp.bfloat16) for part in split_in_three(left)]
    right_high, right_middle, right_low = [part.astype(jnp.bfloat16) for part in split_in_three(right)]
    first = dot_bf16(jnp.concatenate([high, middle, low], axis=0), right_high)
    second = dot_bf16(jnp.concatenate([high, middle], axis=0), right_middle)
    third = dot_bf16(high, right_low)
    small = first[2 * rows :] + (second[rows:] + third)
    return first[:rows] + (first[rows : 2 * rows] + second[:rows] + small)


def solve_with_factors(systems):
    size, width = systems[0].shape
    lanes = 128
    sub = lax.broadcasted_iota(jnp.int32, (BLOCK, lanes), 0)

    def wide(value):
        return jnp.concatenate([value] * (width // lanes), axis=1)

    def spread_row(value, j):
        return jnp.broadcast_to(value[j : j + 1], value.shape)

    def spread_columns(value, start):
        return [
            jnp.broadcast_to(value[:, start + k : start + k + 1], (BLOCK, lanes)) for k in range(BLOCK)
        ]

    total = range(len(systems))
    panel = [system[:BLOCK] for system in systems]
    rest = [system[BLOCK:] for system in systems]
    done = [[] for _ in total]
    for start in range(0, size, BLOCK):
        after = start + BLOCK
        last = after == size
        columns = [spread_columns(panel[i], start) for i in total]
        if not last:
            following = [rest[i][:BLOCK] for i in total]
            next_columns = [spread_columns(following[i], start) for i in total]
        scale = [None for _ in total]
        for j in range(BLOCK):
            for i in total:
                own = columns[i]
                root = lax.rsqrt(spread_row(own[j], j))
                inverse = root * root
                for k in range(j + 1, BLOCK):
                    ratio = spread_row(own[j], k) * inverse
                    own[k] = own[k] - own[j] * ratio
                    if not last:
                        next_columns[i][k] = next_columns[i][k] - next_columns[i][j] * ratio
                pivot_row = spread_row(panel[i], j) * wide(inverse)
                if j < BLOCK - 1:
                    panel[i] = panel[i] - wide(jnp.where(sub > j, own[j], 0.0)) * pivot_row
                if not last:
                    following[i] = following[i] - wide(next_columns[i][j]) * pivot_row
                scale[i] = root if scale[i] is None else jnp.where(sub == j, root, scale[i])
        for i in total:
            solved = panel[i] * wide(scale[i])
            done[i].append(solved[:, lanes:])
            if last:
                continue
            panel[i] = following[i]
            if after + BLOCK < size:
                high, middle, low = split_in_three(solved)
                left = jnp.concatenate(
                    [part[:, :lanes] for part in (high, high, middle, high, middle, low)], axis=0
                )
                left = left.T[after + BLOCK : size].astype(jnp.bfloat16)
                right = jnp.concatenate([high, middle, high, low, middle, high], axis=0)
                rest[i] = rest[i][BLOCK:] - dot_bf16(left, right.astype(jnp.bfloat16))
    return [jnp.concatenate(rows, axis=0) for rows in done]


def store_rows(rows_ref, rows):
    if len(rows_ref.shape) == 2:
        rows_ref[...] = rows
    else:
        for copy in range(rows_ref.shape[0]):
            rows_ref[copy] = rows


def rows_and_weights(copies):
    shape = (RANK, FRAMES) if copies == 1 else (copies, RANK, FRAMES)
    return dict(
        out_specs=[vmem, vmem],
        out_shape=[pltpu.VMEM(shape, jnp.float32), pltpu.VMEM((RANK, FRAMES), jnp.float32)],
    )


def basis_kernel(covariance_ref, test_ref, rows_ref, weights_ref):
    covariance = covariance_ref[...] * (1.0 / (ROWS_DEV * COLS))
    largest = jnp.max(jnp.max(covariance, axis=0, keepdims=True), axis=1, keepdims=True)
    root = lax.rsqrt(largest)
    covariance = covariance * root * root
    sketch = exact_dot(covariance, test_ref[...])
    image = exact_dot(covariance, sketch)
    turned = sketch.T[:RANK]
    system = exact_dot(turned, jnp.concatenate([image, covariance], axis=1))
    (solved,) = solve_with_factors([jnp.concatenate([system, turned], axis=1)])
    store_rows(rows_ref, solved[:, :FRAMES] * (largest * root))
    weights_ref[...] = solved[:, FRAMES:] * root


def tile_basis(covariance, test_matrix, copies=1):
    return pl.pallas_call(
        basis_kernel, in_specs=[vmem, vmem], name="basis", **rows_and_weights(copies)
    )(*near(covariance, test_matrix))


def merge_nodes(stacks, placed, probe):
    systems = []
    for stacked, weights in zip(stacks, placed):
        sketch = exact_dot(stacked, exact_dot(stacked.T, probe))
        systems.append(exact_dot(sketch.T[:RANK], jnp.concatenate([sketch, stacked, weights], axis=1)))
    solved = solve_with_factors(systems)
    rows = [result[:, :FRAMES] * reduction_multiplier for result in solved]
    weights = sum([result[:, FRAMES:] for result in solved[1:]], solved[0][:, FRAMES:])
    return rows, weights * growth_multiplier


def place(weights, first, second):
    return jnp.concatenate([jnp.where(first, weights, 0.0), jnp.where(second, weights, 0.0)], axis=0)


def merge_kernel(place_ref, own_ref, partner_ref, weights_ref, probe_ref, rows_ref, new_weights_ref):
    is_first = place_ref[0] == 0
    own = own_ref[...]
    partner = partner_ref[...]
    stacked = jnp.concatenate([jnp.where(is_first, own, partner), jnp.where(is_first, partner, own)], axis=0)
    placed = place(weights_ref[...], is_first, jnp.logical_not(is_first))
    (rows,), weights = merge_nodes([stacked], [placed], probe_ref[...])
    store_rows(rows_ref, rows)
    new_weights_ref[...] = weights


def merge(place_in, own, partner, weights, probe, copies=1):
    return pl.pallas_call(
        merge_kernel, in_specs=[smem, vmem, vmem, vmem, vmem], name="merge", **rows_and_weights(copies)
    )(place_in, *near(own, partner, weights, probe))


def merge_four_kernel(place_ref, rows_in_ref, weights_ref, probe_ref, rows_ref, new_weights_ref):
    spot = place_ref[0]
    probe = probe_ref[...]
    weights = weights_ref[...]
    stacks = [rows_in_ref[2 * m : 2 * m + 2].reshape(2 * RANK, FRAMES) for m in range(2)]
    placed = [place(weights, spot == 2 * m, spot == 2 * m + 1) for m in range(2)]
    rows, weights = merge_nodes(stacks, placed, probe)
    (rows,), weights = merge_nodes([jnp.concatenate(rows, axis=0)], [place(weights, spot < 2, spot >= 2)], probe)
    store_rows(rows_ref, rows)
    new_weights_ref[...] = weights


def merge_four(place_in, gathered, weights, probe):
    return pl.pallas_call(
        merge_four_kernel, in_specs=[smem, vmem, vmem, vmem], name="merge_four", **rows_and_weights(1)
    )(place_in, *near(gathered, weights, probe))


def sum_over_tm(partial):
    parts = lax.axis_size("tm")
    height = partial.shape[0] // parts
    pieces = lax.all_to_all(partial.reshape(parts, height, -1), "tm", 0, 0, tiled=True)
    own = jnp.sum(pieces, axis=0, keepdims=True)
    whole = lax.all_to_all(jnp.broadcast_to(own, pieces.shape), "tm", 0, 0, tiled=True)
    return whole.reshape(partial.shape)


def body(movie_frames, depth_index, depth_width, temporal_test_matrix, merge_probe):
    frames = movie_frames.shape[0]
    parts = lax.axis_size("tm")
    count = lax.axis_size("pix")
    forward = [(i, i + 1) for i in range(count - 1)]
    backward = [(target, source) for source, target in forward]
    low = lax.ppermute(movie_frames[:, ROWS_DEV - HW :].reshape(frames * HW, COLS), "pix", forward)
    high = lax.ppermute(movie_frames[:, :HW].reshape(frames * HW, COLS), "pix", backward)
    matrices = smoothing_matrices(row_weights(depth_index, depth_width), frames)
    smoothed = smooth_tile(movie_frames, low, high, matrices, parts)
    columns = lax.all_to_all(smoothed, "tm", 0, 0, tiled=True)
    covariance = sum_over_tm(covariance_part(columns))
    spare = FRAMES - RANK
    test_matrix = jnp.pad(temporal_test_matrix, ((0, 0), (0, spare)))
    probe = jnp.pad(merge_probe, ((0, 0), (0, spare)))
    position = lax.axis_index("pix").astype(jnp.int32)
    levels = count.bit_length() - 1
    rows, weights = tile_basis(covariance, test_matrix)
    for level in range(levels - 2):
        pairs = [(source, source ^ (1 << level)) for source in range(count)]
        partner = lax.ppermute(rows, "pix", pairs)
        spot = (position >> level & 1).reshape(1)
        rows, weights = merge(spot, rows, partner, weights, probe, 4 if level == levels - 3 else 1)
    step = count // 4
    groups = [[base + k * step for k in range(4)] for base in range(step)]
    gathered = lax.all_to_all(rows, "pix", 0, 0, tiled=True, axis_index_groups=groups)
    rows, weights = merge_four((position // step).reshape(1), gathered, weights, probe)
    span = lax.axis_index("tm").astype(jnp.int32).reshape(1)
    loadings, own_times = loading_rows(span, rows, weights, columns)
    return (own_times.T, loadings)


def solution(mesh):
    in_specs = (P("tm", "pix", None), P("pix"), P(), P(), P())
    out_specs = (P(None, "tm"), P(None, "pix", "tm"))
    return jax.shard_map(body, mesh=mesh, in_specs=in_specs, out_specs=out_specs, check_vma=False)
```

```python
import math

import jax
import jax.numpy as jnp
from jax import lax
from jax.experimental import pallas as pl
from jax.experimental.pallas import tpu as pltpu
from jax.sharding import PartitionSpec as P

ROWS_DEV = 32
COLS = 4096
FRAMES = 128
RANK = 96
HW = 4
NDEPTH = 6
BLOCK = 8
SMOOTH_GROUP = 4
PAIR_GROUP = 16
LOADING_ROWS = 16

highest = lax.Precision.HIGHEST
reduction_multiplier = math.sqrt(0.5)
growth_multiplier = math.sqrt(2.0)
vmem = pl.BlockSpec(memory_space=pltpu.VMEM)
smem = pl.BlockSpec(memory_space=pltpu.SMEM)


def near(*values):
    return [pltpu.with_memory_space_constraint(value, pltpu.VMEM) for value in values]


def taps_table(depth_width):
    offsets = jnp.arange(-HW, HW + 1).astype(jnp.float32)
    kernel_raw = jnp.exp(-offsets[None, :] ** 2 / (2.0 * depth_width[:, None] ** 2))
    return kernel_raw / jnp.sum(kernel_raw, axis=1, keepdims=True)


def row_weights(row_depth, depth_width):
    classes = jnp.arange(NDEPTH)
    onehot = (row_depth[:, None] == classes[None, :]).astype(jnp.float32)
    return jnp.dot(onehot, taps_table(depth_width), precision=highest)


def split_bf16(value):
    high = lax.reduce_precision(value, exponent_bits=8, mantissa_bits=7)
    return high.astype(jnp.bfloat16), (value - high).astype(jnp.bfloat16)


def smoothing_matrices(weights, frames):
    def matrix(spread, out_row, out_frame, in_row, in_frame):
        tap = jnp.where(in_frame[None, :] == out_frame[:, None], in_row[None, :] - out_row[:, None], -1)
        total = jnp.zeros(tap.shape, jnp.float32)
        for offset in range(2 * HW + 1):
            total = total + jnp.where(tap == offset, spread[:, offset : offset + 1], 0.0)
        high, low = split_bf16(total)
        return jnp.concatenate([high, low], axis=0)

    index = jnp.arange(frames * ROWS_DEV)
    own = matrix(
        jnp.repeat(weights, frames, axis=0),
        index // frames,
        index % frames,
        index % ROWS_DEV + HW,
        index // ROWS_DEV,
    )
    index = jnp.arange(frames * HW)
    edge_rows = index // frames
    sides = [
        matrix(
            jnp.repeat(weights[first : first + HW], frames, axis=0),
            edge_rows + first,
            index % frames,
            index % HW + (first + 2 * HW if first else 0),
            index // HW,
        )
        for first in (0, ROWS_DEV - HW)
    ]
    return own, jnp.concatenate(sides, axis=0)


def dot_bf16(left, right):
    return lax.dot_general(left, right, (((1,), (0,)), ((), ())), preferred_element_type=jnp.float32)


def smooth_kernel(movie_ref, own_ref, out_ref, edges_ref):
    frames, rows, _ = movie_ref.shape
    count, out_rows, width = out_ref.shape
    edge = edges_ref.shape[1] // 2
    start = pl.program_id(0) * count
    own = own_ref[...]
    for part in range(count):
        movie = movie_ref[:, :, part * width : (part + 1) * width].reshape(frames * rows, width)
        both = dot_bf16(own, movie)
        total = both[:out_rows] + both[out_rows:]
        out_ref[part] = total.astype(jnp.bfloat16)
        edges_ref[start + part, :edge] = total[:edge]
        edges_ref[start + part, edge:] = total[out_rows - edge :]


def edge_kernel(_, edges_ref, low_ref, high_ref, matrix_ref, out_ref):
    count, edge, width = out_ref.shape
    side = pl.program_id(0)
    rows = pl.ds(pl.multiple_of(side * edge, edge), edge)
    matrix = matrix_ref[pl.ds(pl.multiple_of(side * 2 * edge, 2 * edge), 2 * edge), :]
    for part in range(count):
        lanes = slice(part * width, (part + 1) * width)
        halo = jnp.where(side == 0, low_ref[:, lanes], high_ref[:, lanes])
        both = dot_bf16(matrix, halo)
        out_ref[part] = (edges_ref[part, rows, :] + (both[:edge] + both[edge:])).astype(jnp.bfloat16)


def smooth_tile(movie, low, high, matrices, parts):
    frames = movie.shape[0]
    width = COLS // parts
    rows = frames * ROWS_DEV
    edge = frames * HW
    group = SMOOTH_GROUP
    own, sides = matrices
    shape = jax.ShapeDtypeStruct((parts, rows, width), jnp.bfloat16)
    smoothed, edges = pl.pallas_call(
        smooth_kernel,
        grid=(parts // group,),
        in_specs=[pl.BlockSpec((frames, ROWS_DEV, group * width), lambda i: (0, 0, i)), vmem],
        out_specs=[pl.BlockSpec((group, rows, width), lambda i: (i, 0, 0)), vmem],
        out_shape=[shape, pltpu.VMEM((parts, 2 * edge, width), jnp.float32)],
        name="smooth",
    )(movie, *near(own))
    return pl.pallas_call(
        edge_kernel,
        grid=(2,),
        in_specs=[pl.BlockSpec(memory_space=pl.ANY), vmem, vmem, vmem, vmem],
        out_specs=pl.BlockSpec((parts, edge, width), lambda i: (0, i * (rows // edge - 1), 0)),
        out_shape=shape,
        input_output_aliases={0: 0},
        name="edges",
    )(smoothed, *near(edges, low, high, sides))


def spread_selector(parity, frames):
    row = lax.broadcasted_iota(jnp.int32, (2 * FRAMES, FRAMES), 0)
    col = lax.broadcasted_iota(jnp.int32, (2 * FRAMES, FRAMES), 1)
    wanted = col // frames * (2 * frames) + parity * frames + col % frames
    return row == wanted


def covariance_kernel(data_ref, out_ref, total_ref):
    step = pl.program_id(0)
    parts, rows, width = data_ref.shape
    pair = rows // PAIR_GROUP
    frames = pair // 2

    @pl.when(step == 0)
    def _():
        total_ref[...] = jnp.zeros_like(total_ref)

    pieces = [
        data_ref[:, i * pair : (i + 1) * pair, :].reshape(parts * pair, width) for i in range(PAIR_GROUP)
    ]
    data = jnp.concatenate(pieces, axis=1)
    total_ref[...] += lax.dot_general(data, data, (((1,), (1,)), ((), ())), preferred_element_type=jnp.float32)

    @pl.when(step == pl.num_programs(0) - 1)
    def _():
        total = total_ref[...].reshape(parts, 2, frames, parts * pair)
        result = None
        for parity in range(2):
            rows = total[:, parity].reshape(parts * frames, parts * pair)
            selector = jnp.where(spread_selector(parity, frames), 1.0, 0.0)
            term = jnp.dot(rows, selector, precision=highest, preferred_element_type=jnp.float32)
            result = term if result is None else result + term
        out_ref[...] = result


def covariance_part(columns):
    parts, rows, width = columns.shape
    block = PAIR_GROUP * 2 * rows // ROWS_DEV
    return pl.pallas_call(
        covariance_kernel,
        grid=(rows // block,),
        in_specs=[pl.BlockSpec((parts, block, width), lambda i: (0, i, 0))],
        out_specs=pl.BlockSpec((FRAMES, FRAMES), lambda i: (0, 0)),
        out_shape=pltpu.VMEM((FRAMES, FRAMES), jnp.float32),
        scratch_shapes=[pltpu.VMEM((2 * FRAMES, 2 * FRAMES), jnp.float32)],
        name="covariance",
    )(columns)


def loading_kernel(
    span_ref, rows_ref, weights_ref, data_ref, out_ref, times_ref, matrix_ref, turn_ref, times_all_ref
):
    rank, height, width = out_ref.shape
    parts, rows, _ = data_ref.shape
    frames = rows // height
    pair = 2 * frames

    @pl.when(pl.program_id(0) == 0)
    def _():
        weights = weights_ref[...].astype(jnp.bfloat16)
        for parity in range(2):
            selector = jnp.where(spread_selector(parity, frames), 1.0, 0.0).astype(jnp.bfloat16)
            spread = lax.dot_general(
                weights, selector, (((1,), (1,)), ((), ())), preferred_element_type=jnp.float32
            )
            matrix_ref[parity * rank : (parity + 1) * rank, :] = spread.astype(jnp.bfloat16)
        times_all_ref[...] = rows_ref[...].T
        times_ref[...] = times_all_ref[pl.ds(pl.multiple_of(span_ref[0] * frames, frames), frames), :]

    matrix = matrix_ref[...]
    for i in range(height // 2):
        data = data_ref[:, i * pair : (i + 1) * pair, :].reshape(parts * pair, width)
        result = dot_bf16(matrix, data)
        for parity in range(2):
            for half in range(width // 128):
                lanes = slice(half * 128, (half + 1) * 128)
                turn_ref[half, pl.ds(2 * i + parity, rank, stride=height), :] = result[
                    parity * rank : (parity + 1) * rank, lanes
                ]
    for half in range(width // 128):
        lanes = slice(half * 128, (half + 1) * 128)
        out_ref[:, :, lanes] = turn_ref[half].reshape(rank, height, 128).astype(jnp.bfloat16)


def loading_rows(span, root_rows, weights, columns):
    parts, rows, width = columns.shape
    height = LOADING_ROWS
    frames = rows // ROWS_DEV
    return pl.pallas_call(
        loading_kernel,
        grid=(ROWS_DEV // height,),
        in_specs=[smem, vmem, vmem, pl.BlockSpec((parts, height * frames, width), lambda i: (0, i, 0))],
        out_specs=[
            pl.BlockSpec((RANK, height, width), lambda i: (0, i, 0)),
            pl.BlockSpec((frames, RANK), lambda i: (0, 0)),
        ],
        out_shape=[
            jax.ShapeDtypeStruct((RANK, ROWS_DEV, width), jnp.bfloat16),
            jax.ShapeDtypeStruct((frames, RANK), jnp.float32),
        ],
        scratch_shapes=[
            pltpu.VMEM((2 * RANK, 2 * FRAMES), jnp.bfloat16),
            pltpu.VMEM((width // 128, RANK * height, 128), jnp.float32),
            pltpu.VMEM((FRAMES, RANK), jnp.float32),
        ],
        name="loadings",
    )(span, *near(root_rows, weights), columns)


def split_in_three(value):
    high = value.astype(jnp.bfloat16).astype(jnp.float32)
    rest = value - high
    middle = rest.astype(jnp.bfloat16).astype(jnp.float32)
    return high, middle, rest - middle


def exact_dot(left, right):
    rows = left.shape[0]
    high, middle, low = [part.astype(jnp.bfloat16) for part in split_in_three(left)]
    right_high, right_middle, right_low = [part.astype(jnp.bfloat16) for part in split_in_three(right)]
    first = dot_bf16(jnp.concatenate([high, middle, low], axis=0), right_high)
    second = dot_bf16(jnp.concatenate([high, middle], axis=0), right_middle)
    third = dot_bf16(high, right_low)
    small = first[2 * rows :] + (second[rows:] + third)
    return first[:rows] + (first[rows : 2 * rows] + second[:rows] + small)


def solve_with_factors(systems):
    size, width = systems[0].shape
    lanes = 128
    sub = lax.broadcasted_iota(jnp.int32, (BLOCK, lanes), 0)

    def wide(value):
        return jnp.concatenate([value] * (width // lanes), axis=1)

    def spread_row(value, j):
        return jnp.broadcast_to(value[j : j + 1], value.shape)

    def spread_columns(value, start):
        return [
            jnp.broadcast_to(value[:, start + k : start + k + 1], (BLOCK, lanes)) for k in range(BLOCK)
        ]

    total = range(len(systems))
    panel = [system[:BLOCK] for system in systems]
    rest = [system[BLOCK:] for system in systems]
    done = [[] for _ in total]
    for start in range(0, size, BLOCK):
        after = start + BLOCK
        last = after == size
        columns = [spread_columns(panel[i], start) for i in total]
        if not last:
            following = [rest[i][:BLOCK] for i in total]
            next_columns = [spread_columns(following[i], start) for i in total]
        scale = [None for _ in total]
        for j in range(BLOCK):
            for i in total:
                own = columns[i]
                root = lax.rsqrt(spread_row(own[j], j))
                inverse = root * root
                for k in range(j + 1, BLOCK):
                    ratio = spread_row(own[j], k) * inverse
                    own[k] = own[k] - own[j] * ratio
                    if not last:
                        next_columns[i][k] = next_columns[i][k] - next_columns[i][j] * ratio
                pivot_row = spread_row(panel[i], j) * wide(inverse)
                if j < BLOCK - 1:
                    panel[i] = panel[i] - wide(jnp.where(sub > j, own[j], 0.0)) * pivot_row
                if not last:
                    following[i] = following[i] - wide(next_columns[i][j]) * pivot_row
                scale[i] = root if scale[i] is None else jnp.where(sub == j, root, scale[i])
        for i in total:
            solved = panel[i] * wide(scale[i])
            done[i].append(solved[:, lanes:])
            if last:
                continue
            panel[i] = following[i]
            if after + BLOCK < size:
                high, middle, low = split_in_three(solved)
                left = jnp.concatenate(
                    [part[:, :lanes] for part in (high, high, middle, high, middle, low)], axis=0
                )
                left = left.T[after + BLOCK : size].astype(jnp.bfloat16)
                right = jnp.concatenate([high, middle, high, low, middle, high], axis=0)
                rest[i] = rest[i][BLOCK:] - dot_bf16(left, right.astype(jnp.bfloat16))
    return [jnp.concatenate(rows, axis=0) for rows in done]


def store_rows(rows_ref, rows):
    if len(rows_ref.shape) == 2:
        rows_ref[...] = rows
    else:
        for copy in range(rows_ref.shape[0]):
            rows_ref[copy] = rows


def rows_and_weights(copies):
    shape = (RANK, FRAMES) if copies == 1 else (copies, RANK, FRAMES)
    return dict(
        out_specs=[vmem, vmem],
        out_shape=[pltpu.VMEM(shape, jnp.float32), pltpu.VMEM((RANK, FRAMES), jnp.float32)],
    )


def basis_kernel(covariance_ref, test_ref, rows_ref, weights_ref):
    covariance = covariance_ref[...] * (1.0 / (ROWS_DEV * COLS))
    largest = jnp.max(jnp.max(covariance, axis=0, keepdims=True), axis=1, keepdims=True)
    root = lax.rsqrt(largest)
    covariance = covariance * root * root
    sketch = exact_dot(covariance, test_ref[...])
    image = exact_dot(covariance, sketch)
    turned = sketch.T[:RANK]
    system = exact_dot(turned, jnp.concatenate([image, covariance], axis=1))
    (solved,) = solve_with_factors([jnp.concatenate([system, turned], axis=1)])
    store_rows(rows_ref, solved[:, :FRAMES] * (largest * root))
    weights_ref[...] = solved[:, FRAMES:] * root


def tile_basis(covariance, test_matrix, copies=1):
    return pl.pallas_call(
        basis_kernel, in_specs=[vmem, vmem], name="basis", **rows_and_weights(copies)
    )(*near(covariance, test_matrix))


def merge_nodes(stacks, placed, probe):
    systems = []
    for stacked, weights in zip(stacks, placed):
        sketch = exact_dot(stacked, exact_dot(stacked.T, probe))
        systems.append(exact_dot(sketch.T[:RANK], jnp.concatenate([sketch, stacked, weights], axis=1)))
    solved = solve_with_factors(systems)
    rows = [result[:, :FRAMES] * reduction_multiplier for result in solved]
    weights = sum([result[:, FRAMES:] for result in solved[1:]], solved[0][:, FRAMES:])
    return rows, weights * growth_multiplier


def place(weights, first, second):
    return jnp.concatenate([jnp.where(first, weights, 0.0), jnp.where(second, weights, 0.0)], axis=0)


def merge_kernel(place_ref, own_ref, partner_ref, weights_ref, probe_ref, rows_ref, new_weights_ref):
    is_first = place_ref[0] == 0
    own = own_ref[...]
    partner = partner_ref[...]
    stacked = jnp.concatenate([jnp.where(is_first, own, partner), jnp.where(is_first, partner, own)], axis=0)
    placed = place(weights_ref[...], is_first, jnp.logical_not(is_first))
    (rows,), weights = merge_nodes([stacked], [placed], probe_ref[...])
    store_rows(rows_ref, rows)
    new_weights_ref[...] = weights


def merge(place_in, own, partner, weights, probe, copies=1):
    return pl.pallas_call(
        merge_kernel, in_specs=[smem, vmem, vmem, vmem, vmem], name="merge", **rows_and_weights(copies)
    )(place_in, *near(own, partner, weights, probe))


def merge_four_kernel(place_ref, rows_in_ref, weights_ref, probe_ref, rows_ref, new_weights_ref):
    spot = place_ref[0]
    probe = probe_ref[...]
    weights = weights_ref[...]
    stacks = [rows_in_ref[2 * m : 2 * m + 2].reshape(2 * RANK, FRAMES) for m in range(2)]
    placed = [place(weights, spot == 2 * m, spot == 2 * m + 1) for m in range(2)]
    rows, weights = merge_nodes(stacks, placed, probe)
    (rows,), weights = merge_nodes([jnp.concatenate(rows, axis=0)], [place(weights, spot < 2, spot >= 2)], probe)
    store_rows(rows_ref, rows)
    new_weights_ref[...] = weights


def merge_four(place_in, gathered, weights, probe):
    return pl.pallas_call(
        merge_four_kernel, in_specs=[smem, vmem, vmem, vmem], name="merge_four", **rows_and_weights(1)
    )(place_in, *near(gathered, weights, probe))


def sum_over_tm(partial):
    parts = lax.axis_size("tm")
    height = partial.shape[0] // parts
    pieces = lax.all_to_all(partial.reshape(parts, height, -1), "tm", 0, 0, tiled=True)
    own = jnp.sum(pieces, axis=0, keepdims=True)
    whole = lax.all_to_all(jnp.broadcast_to(own, pieces.shape), "tm", 0, 0, tiled=True)
    return whole.reshape(partial.shape)


def body(movie_frames, depth_index, depth_width, temporal_test_matrix, merge_probe):
    frames = movie_frames.shape[0]
    parts = lax.axis_size("tm")
    count = lax.axis_size("pix")
    forward = [(i, i + 1) for i in range(count - 1)]
    backward = [(target, source) for source, target in forward]
    low = lax.ppermute(movie_frames[:, ROWS_DEV - HW :].reshape(frames * HW, COLS), "pix", forward)
    high = lax.ppermute(movie_frames[:, :HW].reshape(frames * HW, COLS), "pix", backward)
    matrices = smoothing_matrices(row_weights(depth_index, depth_width), frames)
    smoothed = smooth_tile(movie_frames, low, high, matrices, parts)
    columns = lax.all_to_all(smoothed, "tm", 0, 0, tiled=True)
    covariance = sum_over_tm(covariance_part(columns))
    spare = FRAMES - RANK
    test_matrix = jnp.pad(temporal_test_matrix, ((0, 0), (0, spare)))
    probe = jnp.pad(merge_probe, ((0, 0), (0, spare)))
    position = lax.axis_index("pix").astype(jnp.int32)
    levels = count.bit_length() - 1
    rows, weights = tile_basis(covariance, test_matrix)
    for level in range(levels - 2):
        pairs = [(source, source ^ (1 << level)) for source in range(count)]
        partner = lax.ppermute(rows, "pix", pairs)
        spot = (position >> level & 1).reshape(1)
        rows, weights = merge(spot, rows, partner, weights, probe, 4 if level == levels - 3 else 1)
    step = count // 4
    groups = [[base + k * step for k in range(4)] for base in range(step)]
    gathered = lax.all_to_all(rows, "pix", 0, 0, tiled=True, axis_index_groups=groups)
    rows, weights = merge_four((position // step).reshape(1), gathered, weights, probe)
    span = lax.axis_index("tm").astype(jnp.int32).reshape(1)
    loadings, own_times = loading_rows(span, rows, weights, columns)
    return (own_times.T, loadings)


def solution(mesh):
    in_specs = (P("tm", "pix", None), P("pix"), P(), P(), P())
    out_specs = (P(None, "tm"), P(None, "pix", "tm"))
    return jax.shard_map(body, mesh=mesh, in_specs=in_specs, out_specs=out_specs, check_vma=False)
```
